128 devices in a mesh: group: 16 (over x, z_hi, core), inner: 8 (over z_lo, y).
Axes of the slice: x: 4, y: 4, z: 4 (z_hi: 2, z_lo: 2; z = z_hi * 2 + z_lo), core: 2. Of those that a mesh axis runs over, the one named last changes fastest.
Arguments:
- tokens: bfloat16 [16, 512, 2304], P('group', 'inner'), may hold values from -6 to 6
- lengths: int32 [16], P('group'), may hold values from 1 to 512, 5120 in all
- tenant_cut: int32 [16], P('group'), may hold values from 64 to 255
- expert_ids: int32 [16, 512, 2], P('group', 'inner'), may hold values from 0 to 7, all different within a row; in each aligned block of 64 rows (0 to 63, 64 to 127, ..., all dimensions but the last counted through in order) at most 20 rows name the same one
- trainer_qkv: float32 [2304, 3, 2048], P(('group', 'inner')), may hold values from -0.26 to 0.26
- trainer_gate_up: float32 [8, 2304, 2, 5760], P(None, ('group', 'inner')), may hold values from -0.125 to 0.125
- out_weight: bfloat16 [2048, 2304], P('inner'), may hold values from -0.75 to 0.75
- down_weight: bfloat16 [8, 5760, 2304], P('inner', 'group'), may hold values from -0.078125 to 0.078125
- attn_gain: float32 [2304], replicated, may hold values from 0.1 to 1.9
- moe_gain: float32 [2304], replicated, may hold values from 0.1 to 1.9
- router: bfloat16 [2304, 8], replicated, may hold values from -0.375 to 0.375
Outputs:
- server_qkv: bfloat16 [2304, 3, 2048], P(None, None, 'inner')
- server_gate_up: bfloat16 [8, 2304, 2, 5760], P('inner', None, None, 'group')
- layer_out: bfloat16 [16, 512, 2304], P('group', 'inner')
The draws below stay inside these ranges and needn't reach their ends.
Inputs may be any that keep to these rules, and one draw needn't show every extreme that they name: `expert_ids`: in each aligned block of 64 token slots (the slots of one device) no expert is named more than 20 times, a bound that some block reaches. The two experts of a slot differ. `lengths`: some prompt uses all 512 slots.
All inputs are finite; a program needn't handle non-finite values. No bound on the sum of `lengths` on one device may be relied on, other than what follows from the above.
Results may differ from the reference program's by a relative error of at most 0.015.
Values may be sent and summed in bfloat16 or wider, within the bound.
A program may use at most 128 MiB of HBM per device.

```python
import math
import jax
import jax.numpy as jnp
import numpy as np
from jax import lax

D = 2304
HEADS = 32
HEAD_DIM = 64
EXPERTS = 8
FF = 5760
TOPK = 2
SEQ = 512
PROMPTS = 16
TOK_DEV = 64
CAP = 20
FF_DEV = 360
N_GROUP = 16
N_INNER = 8


QKV_SCALE = 1.0 / 48.0


def draw_trainer_qkv(key, part):
    shape_all = (D, 3, HEADS * HEAD_DIM)
    base = jax.random.normal(key, shape_all, jnp.float32) * QKV_SCALE
    return jnp.clip(base, -6.0 * QKV_SCALE, 6.0 * QKV_SCALE)


def set_ends(entries, own_key, low, top_value):
    longest = entries.shape.index(max(entries.shape))
    spots = []
    for shift in (0, 1):
        where = [jax.random.randint(jax.random.fold_in(own_key, axis), (), 0, length) for axis, length in enumerate(entries.shape)]
        where[longest] = (where[longest] + shift) % entries.shape[longest]
        spots.append(tuple(where))
    return entries.at[spots[0]].set(low).at[spots[1]].set(top_value)


def levels(rng, shape, shards, smallest, high):
    gain, own = 1.0, jax.random.fold_in(rng, 6)
    for dim, shards_of in shards:
        steps = jnp.exp(jax.random.uniform(jax.random.fold_in(own, dim), (shards_of,), jnp.float32, smallest / len(shards), high / len(shards)))
        gain = gain * jnp.repeat(steps, shape[dim] // shards_of).reshape([-1 if axis == dim else 1 for axis in range(len(shape))])
    return gain


def split_up(count, total, most, skew):
    loads = [(1 << 20) // math.isqrt(grade ** skew) + 1 for grade in range(2, count + 1)]
    rest, given = total - most - (count - 1), [1] * (count - 1)
    while rest > 0:
        candidates = [i for i in range(count - 1) if given[i] < most]
        mass, left = sum([loads[i] for i in candidates]), rest
        for i in candidates:
            extra = min(most - given[i], max(1, left * loads[i] // mass), rest)
            given[i] = given[i] + extra
            rest = rest - extra
    return np.array([most] + given)


def ragged_sizes(key, number_of, total, limit, lean):
    if number_of == 2:
        one = jax.random.randint(key, (), max(1, total - limit), min(limit, total - 1) + 1)
        return jnp.stack([one, total - one])
    sizes = jnp.asarray(split_up(number_of, total, limit, lean), jnp.int32)
    twos = (number_of - 1) // 2
    source_of, taker = sizes[1:1 + 2 * twos:2], sizes[2:2 + 2 * twos:2]
    room = jnp.minimum(source_of - 1, limit - taker)
    moved = jax.random.randint(jax.random.fold_in(key, 1), (twos,), 0, 1 << 20) % (room + 1)
    sizes = sizes.at[1:1 + 2 * twos:2].set(source_of - moved).at[2:2 + 2 * twos:2].set(taker + moved)
    return sizes[jax.random.permutation(jax.random.fold_in(key, 2), number_of)]


def assign_block(stream_key, own, number, rows, amount, top, bound, slope):
    ranking = jax.random.permutation(stream_key, amount)
    heavy_load, usual = shares(amount, rows * top, bound, slope, True), shares(amount, rows * top, bound, slope, False)
    places = jnp.arange(amount)

    def named(tallies, turn):
        used = int((tallies > 0).sum())
        fixed = max(1, used // 4)
        moved = fixed + (places - fixed + turn * (used - fixed)) % max(1, amount - fixed)
        return jnp.zeros((amount,), jnp.int32).at[ranking[jnp.where(places < fixed, places, moved)]].set(jnp.asarray(tallies, jnp.int32))

    tallies = jnp.where(number % 4 == 0, named(heavy_load, number // 4), named(usual, number - number // 4 - 1))
    mixed = jax.random.permutation(jax.random.fold_in(own, 3), amount)
    source_of, sink = mixed[0:amount // 2 * 2:2], mixed[1:amount // 2 * 2:2]
    room = jnp.minimum(tallies[source_of] - 1, bound - tallies[sink]) // 2
    room = jnp.where((source_of == ranking[0]) | (sink == ranking[0]) | (tallies[sink] == 0), 0, jnp.maximum(room, 0))
    moved = jax.random.randint(jax.random.fold_in(own, 4), (amount // 2,), 0, 1 << 20) % (room + 1)
    tallies = tallies.at[source_of].add(-moved).at[sink].add(moved)
    members = jnp.searchsorted(jnp.cumsum(tallies), jnp.arange(rows * top), side="right").astype(jnp.int32)
    listing = members.reshape(top, rows).T
    listing = listing[jax.random.permutation(jax.random.fold_in(own, 1), rows)]
    turn = jax.random.randint(jax.random.fold_in(own, 2), (rows, 1), 0, top)
    return jnp.take_along_axis(listing, (jnp.arange(top)[None, :] + turn) % top, axis=1)


def shares(number_of, total, reach, slope, full):
    loads = [(1 << 20) // math.isqrt(grade ** slope) + 1 for grade in range(1, number_of + 1)]
    largest = reach if full else min(reach, max(-(-total // number_of), total * loads[0] // sum(loads)))
    least = 1 if total - largest >= number_of - 1 else 0
    holding, surplus = [largest] + [least] * (number_of - 1), total - largest - least * (number_of - 1)
    while surplus > 0:
        movable = [i for i in range(1, number_of) if holding[i] < largest] or [i for i in range(1, number_of) if holding[i] < reach]
        mass, budget = sum([loads[i] for i in movable]), surplus
        for i in movable:
            extra = min(reach - holding[i], max(1, budget * loads[i] // mass), surplus)
            holding[i] = holding[i] + extra
            surplus = surplus - extra
    return np.array(holding)


def noise(stream_key, dims, deviation, most, split=(), kind=jnp.bfloat16):
    values = deviation * jax.random.normal(stream_key, dims, jnp.float32)
    if split:
        values = values * levels(stream_key, dims, split, -0.22, 0.18)
    return jnp.clip(values, -most, most).astype(kind)


def setup_inputs(seed: int = 0) -> dict:
    key_of = jax.random.split(jax.random.key(seed), 12)
    tokens = noise(key_of[0], (PROMPTS, SEQ, D), 1.0, 6.0, ((0, 16), (1, 8)))
    lengths = ragged_sizes(key_of[1], PROMPTS, PROMPTS * SEQ * 5 // 8, SEQ, 1).astype(jnp.int32)
    tenant_cut = set_ends(jax.random.randint(key_of[2], (PROMPTS,), SEQ // 8, SEQ // 2), jax.random.fold_in(key_of[2], 1), SEQ // 8, (SEQ // 2) - 1).astype(jnp.int32)
    expert_ids_keys = jax.random.split(jax.random.fold_in(key_of[3], 1), PROMPTS * SEQ // TOK_DEV)
    expert_ids_turns = jax.random.permutation(jax.random.fold_in(key_of[3], 3), PROMPTS * SEQ // TOK_DEV)
    expert_ids = jax.vmap(lambda own, number: assign_block(jax.random.fold_in(key_of[3], 2), own, number, TOK_DEV, EXPERTS, TOPK, CAP, 1))(expert_ids_keys, expert_ids_turns).reshape((PROMPTS, SEQ, TOPK))
    trainer_qkv = draw_trainer_qkv(jax.random.fold_in(key_of[11], 71), 0)
    trainer_gate_up = noise(key_of[5], (EXPERTS, D, 2, FF), D ** -0.5, 0.125, ((1, 128),), jnp.float32)
    out_weight = noise(key_of[6], (HEADS * HEAD_DIM, D), (HEADS * HEAD_DIM // 32) ** -0.5, 0.75, ((0, 8),))
    down_weight = noise(key_of[7], (EXPERTS, FF, D), FF ** -0.5, 0.078125, ((0, 8), (1, 16)))
    attn_gain = jnp.clip(1.0 + 0.18 * jax.random.normal(key_of[8], (D,), jnp.float32), 0.1, 1.9)
    moe_gain = jnp.clip(1.0 + 0.18 * jax.random.normal(key_of[9], (D,), jnp.float32), 0.1, 1.9)
    router = noise(key_of[10], (D, EXPERTS), (D // 8) ** -0.5, 0.375)
    return dict(tokens=tokens, lengths=lengths, tenant_cut=tenant_cut, expert_ids=expert_ids, trainer_qkv=trainer_qkv, trainer_gate_up=trainer_gate_up, out_weight=out_weight, down_weight=down_weight, attn_gain=attn_gain, moe_gain=moe_gain, router=router)


NORM_EPS = 1e-05
MASKED = -1e+30

def rms_scaled(values, gain_row):
    mean_square = lax.optimization_barrier(jnp.mean(values * values, axis=-1, keepdims=True))
    return values * lax.rsqrt(mean_square + NORM_EPS) * gain_row

def token_layout(length, cut_point, offset, total):
    places = offset + jnp.arange(total, dtype=jnp.int32)
    beyond = places >= length
    second = places >= cut_point
    starts = jnp.where(beyond, length, jnp.where(second, cut_point, 0))
    tenants = jnp.where(beyond, 2, jnp.where(second, 1, 0))
    return (places - starts, tenants, places)

def rotate_heads(values, positions):
    half_dim = values.shape[-1] // 2
    freqs = jnp.exp(-math.log(10000.0) * jnp.arange(half_dim, dtype=jnp.float32) / half_dim)
    angles = positions.astype(jnp.float32)[:, None] * freqs[None, :]
    cosine = jnp.cos(angles)[:, None, :]
    sine = jnp.sin(angles)[:, None, :]
    first_half = values[..., :half_dim]
    second_half = values[..., half_dim:]
    return jnp.concatenate([first_half * cosine - second_half * sine, second_half * cosine + first_half * sine], axis=-1)

def attend_prompt(normed_rows, flat_qkv, length, cut_point):
    seq_len = normed_rows.shape[0]
    raw = jnp.dot(normed_rows, flat_qkv, preferred_element_type=jnp.float32).reshape(seq_len, 3, HEADS, HEAD_DIM)
    positions, tenants, places = token_layout(length, cut_point, 0, seq_len)
    queries = rotate_heads(raw[:, 0], positions).astype(jnp.bfloat16)
    keys_rot = rotate_heads(raw[:, 1], positions).astype(jnp.bfloat16)
    values_v = raw[:, 2].astype(jnp.bfloat16)
    scores = jnp.einsum('qhd,khd->hqk', queries.astype(jnp.float32), keys_rot.astype(jnp.float32)) / math.sqrt(HEAD_DIM)
    allowed = (tenants[:, None] == tenants[None, :]) & (places[None, :] <= places[:, None])
    scores = jnp.where(allowed[None], scores, MASKED)
    weights = jax.nn.softmax(scores, axis=-1).astype(jnp.bfloat16)
    mixed = jnp.einsum('hqk,khd->qhd', weights.astype(jnp.float32), values_v.astype(jnp.float32))
    return mixed.astype(jnp.bfloat16).reshape(seq_len, HEADS * HEAD_DIM)

def reference(tokens, lengths, tenant_cut, expert_ids, trainer_qkv, trainer_gate_up, out_weight, down_weight, attn_gain, moe_gain, router):
    server_qkv = trainer_qkv.astype(jnp.bfloat16)
    server_gate_up = trainer_gate_up.astype(jnp.bfloat16)
    inputs_f = tokens.astype(jnp.float32)
    normed = rms_scaled(inputs_f, attn_gain).astype(jnp.bfloat16)
    flat_qkv = server_qkv.reshape(D, 3 * HEADS * HEAD_DIM)
    attended = lax.map(lambda packed: attend_prompt(packed[0], flat_qkv, packed[1], packed[2]), (normed, lengths, tenant_cut))
    projected = jnp.dot(attended.reshape(-1, HEADS * HEAD_DIM), out_weight, preferred_element_type=jnp.float32)
    residual = inputs_f.reshape(-1, D) + projected
    normed_moe = rms_scaled(residual, moe_gain).astype(jnp.bfloat16)
    logits = jnp.dot(normed_moe, router, preferred_element_type=jnp.float32)
    route_ids = expert_ids.reshape(-1, TOPK)
    chosen = jnp.take_along_axis(logits, route_ids, axis=1)
    first_weight = jax.nn.sigmoid(chosen[:, 0] - chosen[:, 1])
    route_weights = jnp.stack([first_weight, 1.0 - first_weight], axis=1).reshape(-1)
    flat_ids = route_ids.reshape(-1)
    slot_total = N_GROUP * N_INNER * CAP
    token_total = route_ids.shape[0]

    def expert_step(carry, expert):
        order = jnp.argsort((flat_ids != expert).astype(jnp.int32), stable=True)[:slot_total].astype(jnp.int32)
        valid = flat_ids[order] == expert
        token_rows = (order // TOPK).astype(jnp.int32)
        picked = normed_moe[token_rows]
        gate_up = server_gate_up[expert]
        gate_part = jnp.dot(picked, gate_up[:, 0, :], preferred_element_type=jnp.float32)
        up_part = jnp.dot(picked, gate_up[:, 1, :], preferred_element_type=jnp.float32)
        hidden = (jax.nn.silu(gate_part) * up_part).astype(jnp.bfloat16)
        down_rows = down_weight[expert]

        def add_slice(index, total):
            begin = (index * FF_DEV).astype(jnp.int32)
            hidden_slice = lax.dynamic_slice_in_dim(hidden, begin, FF_DEV, 1)
            down_slice = lax.dynamic_slice_in_dim(down_rows, begin, FF_DEV, 0)
            term = lax.optimization_barrier(jnp.dot(hidden_slice, down_slice, preferred_element_type=jnp.float32).astype(jnp.bfloat16))
            return total + term.astype(jnp.float32)
        summed = lax.fori_loop(jnp.int32(0), jnp.int32(N_GROUP), add_slice, jnp.zeros((slot_total, D), jnp.float32))
        outputs = lax.optimization_barrier(summed.astype(jnp.bfloat16)).astype(jnp.float32)
        scale = jnp.where(valid, route_weights[order], jnp.float32(0.0))
        return (carry.at[token_rows].add(outputs * scale[:, None]), None)
    moe = lax.scan(expert_step, jnp.zeros((token_total, D), jnp.float32), jnp.arange(EXPERTS, dtype=jnp.int32))[0]
    combined = (residual + moe).reshape(PROMPTS, SEQ, D)
    live = jnp.arange(SEQ, dtype=jnp.int32)[None, :] < lengths[:, None]
    layer_out = jnp.where(live[:, :, None], combined, jnp.float32(0.0)).astype(jnp.bfloat16)
    return (server_qkv, server_gate_up, layer_out)
```

```python
import math

import jax
import jax.numpy as jnp
from jax import lax
from jax.experimental import pallas as pl
from jax.experimental.pallas import tpu as pltpu
from jax.sharding import PartitionSpec as P

F32 = jnp.float32
BF16 = jnp.bfloat16
MESH = pl.DeviceIdType.MESH
D = 2304
HEAD_DIM = 64
EPS = 1e-05
MASKED = -1e30
ROWS = 18
FFL = 360
FFP = 384
SLOT = 32
CAP = 20
CH = 80
NC = 2
SEQ = 512
TOK = 64


def remote(src, dst, send_sem, recv_sem, device):
    return pltpu.make_async_remote_copy(
        src_ref=src, dst_ref=dst, send_sem=send_sem, recv_sem=recv_sem, device_id=device, device_id_type=MESH
    )


class Spread:
    SENDS = ((0, 0, "R"), (0, 0, "L"), (0, 0, "P"), (0, 1, "R"), (0, 1, "L"), (3, 0, "R"), (1, 1, "L"))
    LANDS = ((3, 0), (1, 0), (0, 1), (3, 1), (1, 1), (2, 0), (2, 1))

    def __init__(self, block, devices, sems, base, relative):
        self.block, self.devices, self.sems, self.base, self.relative = block, devices, sems, base, relative

    def send(self, k):
        dx, dz, way = self.SENDS[k]
        target = self.LANDS[k] if self.relative else (dx, dz)
        n = self.base + k
        return remote(self.block(dx, dz), self.block(*target), self.sems[0].at[n], self.sems[1].at[n], self.devices[way])

    def start(self, *ks):
        for k in ks:
            self.send(k).start()

    def arrived(self, *ks):
        for k in ks:
            n = self.base + k
            land = self.block(*self.LANDS[k])
            remote(land, land, self.sems[0].at[n], self.sems[1].at[n], self.devices[self.SENDS[k][2]]).wait_recv()

    def drain(self):
        for k in range(7):
            self.send(k).wait_send()


class Gather:
    SENDS = ((2, 0, "L"), (2, 1, "R"), (3, 0, "L"), (1, 1, "R"), (3, 1, "L"), (1, 0, "R"), (0, 1, "P"))

    def __init__(self, block, lands, devices, sems, base):
        self.block, self.lands, self.devices, self.sems, self.base = block, lands, devices, sems, base

    def send(self, k):
        dx, dz, way = self.SENDS[k]
        n = self.base + k
        return remote(self.block(dx, dz), self.lands(k), self.sems[0].at[n], self.sems[1].at[n], self.devices[way])

    def start(self, *ks):
        for k in ks:
            self.send(k).start()

    def arrived(self, *ks):
        for k in ks:
            self.send(k).wait_recv()

    def add(self, dx, dz, *ks):
        ref = self.block(dx, dz)
        total = ref[...].astype(F32)
        for k in ks:
            total = total + self.lands(k)[...].astype(F32)
        ref[...] = total.astype(BF16)

    def middle(self):
        self.arrived(0)
        self.add(3, 0, 0)
        self.start(2)
        self.arrived(1)
        self.add(1, 1, 1)
        self.start(3)

    def cross(self):
        self.arrived(3, 4)
        self.add(0, 1, 3, 4)
        self.start(6)

    def total(self):
        self.arrived(2, 5, 6)
        own = self.block(0, 0)[...].astype(F32) + self.lands(6)[...].astype(F32)
        return own + self.lands(2)[...].astype(F32) + self.lands(5)[...].astype(F32)

    def drain(self):
        for k in range(7):
            self.send(k).wait_send()


def where_am_i():
    g = lax.axis_index("group")
    i = lax.axis_index("inner")
    return g, i, g // 4, (g // 2) % 2, g % 2, i // 4, i % 4


def group_id(x, zh, c):
    return x * 4 + zh * 2 + c


def normalize(values, gain):
    mean_square = jnp.mean(values * values, axis=-1, keepdims=True)
    return values * lax.rsqrt(mean_square + EPS) * gain


def front_kernel(
    len_ref, cut_ref, tok_ref, gain_ref, freq_ref, tq_ref, ow_ref, gu_hbm,
    resid_ref, q3_hbm, wt_hbm,
    gu, sbuf, rbuf, qs, qr, w, xb, qkv, att, pb, r1, r2, rz, wt,
    load_sem, gsend, grecv, qsem_s, qsem_r, xsem_s, xsem_r, wsem_s, wsem_r, csem_s, csem_r, psem_s, psem_r, out_sem,
):
    g, i, x, zh, c, zl, y = where_am_i()
    me = g * 8 + i

    def load(k):
        e = lax.rem(i + k, 8)
        return pltpu.make_async_copy(gu_hbm.at[e], gu.at[k], load_sem.at[k])

    for k in range(8):
        load(k).start()

    barrier = pltpu.get_barrier_semaphore()

    def greet(k, carry):
        t = lax.rem(me + k, 128)
        pl.semaphore_signal(barrier, 1, device_id=(t // 8, t % 8), device_id_type=MESH)
        return carry

    lax.fori_loop(1, 128, greet, 0)

    own_inputs = tok_ref[...].astype(F32)
    xb[i] = normalize(own_inputs, gain_ref[...]).astype(BF16)
    for e in range(8):
        cols = slice(e * 256, (e + 1) * 256)
        slab = jnp.concatenate([tq_ref[:, j, cols] for j in range(3)], axis=-1)
        qs[e] = slab.reshape(9, 2, 768).astype(BF16)
    pl.semaphore_wait(barrier, 127)

    inner_devices = {
        "R": (g, zl * 4 + lax.rem(y + 1, 4)),
        "L": (g, zl * 4 + lax.rem(y + 3, 4)),
        "P": (g, (1 - zl) * 4 + y),
    }
    group_devices = {
        "R": (group_id(lax.rem(x + 1, 4), zh, c), i),
        "L": (group_id(lax.rem(x + 3, 4), zh, c), i),
        "P": (group_id(x, 1 - zh, c), i),
    }

    def inner_slot(dx, dz):
        return (zl if dz == 0 else 1 - zl) * 4 + lax.rem(y + dx, 4)

    def group_slot(dx, dz):
        return group_id(lax.rem(x + dx, 4), zh if dz == 0 else 1 - zh, c)

    tokens_all = Spread(lambda dx, dz: xb.at[inner_slot(dx, dz)], inner_devices, (xsem_s, xsem_r), 0, False)
    proj_all = Spread(lambda dx, dz: w.at[:, group_slot(dx, dz)], group_devices, (wsem_s, wsem_r), 0, False)

    def slab_send(k):
        t = lax.rem(i + k, 8)
        return remote(qs.at[t], qr.at[i], qsem_s.at[k], qsem_r.at[k], (g, t))

    for k in range(1, 8):
        slab_send(k).start()
    tokens_all.start(0, 1, 2)
    qr[i] = qs[i]

    def gate_send(tg, e):
        t = tg * 8 + e
        return remote(sbuf.at[t], rbuf.at[me], gsend.at[t], grecv.at[me], (tg, e))

    def ship(k):
        e = lax.rem(i + k, 8)
        load(k).wait()
        for q in range(16):
            sbuf[q * 8 + e] = gu[k, :, :, q * FFL:(q + 1) * FFL].astype(BF16)

        def post(q, carry):
            tg = lax.rem(g + q, 16)
            gate_send(tg, e).start()
            return carry

        if k == 0:
            rbuf[me] = sbuf[me]
            lax.fori_loop(1, 16, post, 0)
        else:
            lax.fori_loop(0, 16, post, 0)

    ship(0)
    ship(1)
    tokens_all.arrived(2)
    tokens_all.start(3, 4)
    for k in range(1, 8):
        s = lax.rem(i + 8 - k, 8)
        remote(qr.at[s], qr.at[s], qsem_s.at[k], qsem_r.at[k], (g, s)).wait_recv()
    block = qr[...].reshape(72, 2, 768).reshape(144, 768)
    for j in range(3):
        w[j, g] = block[:, j * 256:(j + 1) * 256]
    proj_all.start(0, 1, 2)

    other_core = (group_id(x, zh, 1 - c), i)

    def core_send(k, dx, dz):
        s = group_slot(dx, dz)
        return remote(w.at[:, s], w.at[:, s], csem_s.at[k], csem_r.at[k], other_core)

    def core_land(k, dx, dz):
        s = group_id(lax.rem(x + dx, 4), zh if dz == 0 else 1 - zh, 1 - c)
        return remote(w.at[:, s], w.at[:, s], csem_s.at[k], csem_r.at[k], other_core)

    order = ((0, 0), (0, 1), (3, 0), (1, 0), (3, 1), (1, 1), (2, 0), (2, 1))
    core_send(0, 0, 0).start()
    ship(2)
    tokens_all.arrived(0)
    tokens_all.start(5)
    proj_all.arrived(2)
    proj_all.start(3, 4)
    core_send(1, 0, 1).start()
    ship(3)
    tokens_all.arrived(4)
    tokens_all.start(6)
    proj_all.arrived(0)
    proj_all.start(5)
    core_send(2, 3, 0).start()
    proj_all.arrived(1)
    core_send(3, 1, 0).start()
    ship(4)
    proj_all.arrived(4)
    proj_all.start(6)
    core_send(5, 1, 1).start()
    proj_all.arrived(3)
    core_send(4, 3, 1).start()
    ship(5)
    ship(6)
    ship(7)

    length = len_ref[0]
    cut = cut_ref[0]
    places = lax.broadcasted_iota(jnp.int32, (SEQ, 128), 0)
    starts = jnp.where(places >= length, length, jnp.where(places >= cut, cut, 0))
    angles = (places - starts).astype(F32) * freq_ref[...]
    cosine = jnp.cos(angles)
    lane = lax.broadcasted_iota(jnp.int32, (SEQ, 128), 1)
    early = lane % HEAD_DIM < HEAD_DIM // 2
    sine = jnp.sin(angles)
    sine = jnp.where(early, -sine, sine)

    tokens_all.arrived(1, 3, 5, 6)
    proj_all.arrived(5)
    core_send(6, 2, 0).start()
    proj_all.arrived(6)
    core_send(7, 2, 1).start()
    for k, (dx, dz) in enumerate(order):
        core_land(k, dx, dz).wait_recv()
    q3_copy = pltpu.make_async_copy(w, q3_hbm, out_sem.at[0])
    q3_copy.start()

    rows = xb[...].reshape(SEQ, D)
    for j in range(3):
        raw = jnp.dot(rows, w[j].reshape(D, 256), preferred_element_type=F32)
        if j < 2:
            halves = []
            for n in range(2):
                part = raw[:, n * 128:(n + 1) * 128]
                swapped = jnp.where(early, pltpu.roll(part, 96, 1), pltpu.roll(part, 32, 1))
                halves.append(part * cosine + swapped * sine)
            raw = jnp.concatenate(halves, axis=-1)
        qkv[j] = raw.astype(BF16)

    for r in range(4):
        span = (r + 1) * 128
        t = r * 128 + lax.broadcasted_iota(jnp.int32, (128, span), 0)
        s = lax.broadcasted_iota(jnp.int32, (128, span), 1)
        seg_t = jnp.where(t >= length, 2, jnp.where(t >= cut, 1, 0))
        seg_s = jnp.where(s >= length, 2, jnp.where(s >= cut, 1, 0))
        allowed = (s <= t) & (seg_t == seg_s)
        first = lax.broadcasted_iota(jnp.int32, (128, 128), 1) < HEAD_DIM
        for n in range(2):
            cols = slice(n * 128, (n + 1) * 128)
            q = qkv[0, r * 128:(r + 1) * 128, cols]
            k = qkv[1, :span, cols]
            v = qkv[2, :span, cols]
            mixed = []
            for h in range(2):
                keep = first if h == 0 else jnp.logical_not(first)
                qh = jnp.where(keep, q.astype(F32), 0.0).astype(BF16)
                scores = lax.dot_general(qh, k, (((1,), (1,)), ((), ())), preferred_element_type=F32)
                scores = jnp.where(allowed, scores / math.sqrt(HEAD_DIM), MASKED)
                scores = jnp.exp(scores - jnp.max(scores, axis=-1, keepdims=True))
                weights = (scores / jnp.sum(scores, axis=-1, keepdims=True)).astype(BF16)
                mixed.append(jnp.dot(weights, v, preferred_element_type=F32))
            att[r * 128:(r + 1) * 128, cols] = jnp.where(first, mixed[0], mixed[1]).astype(BF16)

    def project(n, carry):
        cols = pl.ds(pl.multiple_of(n * 256, 256), 256)
        part = jnp.dot(att[...], ow_ref[:, cols], preferred_element_type=F32)
        pb[:, :, cols] = part.astype(BF16).reshape(8, TOK, 256)
        return carry

    lax.fori_loop(0, D // 256, project, 0)

    def land(k):
        return r1.at[k] if k < 2 else (rz if k == 6 else r2.at[k - 2])

    back = Gather(lambda dx, dz: pb.at[inner_slot(dx, dz)], land, inner_devices, (psem_s, psem_r), 0)
    back.start(0, 1, 4, 5)

    def settle(k, carry):
        s = lax.rem(me + k, 128)
        remote(rbuf.at[s], rbuf.at[s], gsend.at[s], grecv.at[s], (s // 8, s % 8)).wait_recv()
        return carry

    wt[:, 352:384, :] = jnp.zeros((2, 32, D), BF16)


    back.middle()
    lax.fori_loop(1, 128, settle, 0)
    flat = rbuf.reshape(128 * ROWS, 2, FFL)

    def turn_step(n, carry):
        cols = pl.ds(pl.multiple_of(n * 256, 256), 256)
        wt[:, :FFL, cols] = jnp.transpose(flat[cols], (1, 2, 0))
        return carry

    lax.fori_loop(0, 4, turn_step, 0)
    back.cross()
    lax.fori_loop(4, 9, turn_step, 0)
    wt_copy = pltpu.make_async_copy(wt, wt_hbm, out_sem.at[1])
    wt_copy.start()
    resid_ref[...] = own_inputs + back.total()

    def sent(k, carry):
        t = lax.rem(me + k, 128)
        gate_send(t // 8, t % 8).wait_send()
        return carry

    lax.fori_loop(1, 128, sent, 0)
    for k in range(1, 8):
        slab_send(k).wait_send()
    tokens_all.drain()
    proj_all.drain()
    back.drain()
    for k, (dx, dz) in enumerate(order):
        core_send(k, dx, dz).wait_send()
    q3_copy.wait()
    wt_copy.wait()


def front(tokens, lengths, cuts, gain, freqs, tq, ow, gu):
    vm = pl.BlockSpec(memory_space=pltpu.VMEM)
    sm = pl.BlockSpec(memory_space=pltpu.SMEM)
    hbm = pl.BlockSpec(memory_space=pl.ANY)
    dma = pltpu.SemaphoreType.DMA
    return pl.pallas_call(
        front_kernel,
        name="front",
        out_shape=(
            jax.ShapeDtypeStruct((TOK, D), F32),
            jax.ShapeDtypeStruct((3, 16, 144, 256), BF16),
            jax.ShapeDtypeStruct((2, FFP, D), BF16),
        ),
        in_specs=[sm, sm, vm, vm, vm, vm, vm, hbm],
        out_specs=(vm, hbm, hbm),
        scratch_shapes=[
            pltpu.VMEM((8, ROWS, 2, 5760), F32),
            pltpu.VMEM((128, ROWS, 2, FFL), BF16),
            pltpu.VMEM((128, ROWS, 2, FFL), BF16),
            pltpu.VMEM((8, 9, 2, 768), BF16),
            pltpu.VMEM((8, 9, 2, 768), BF16),
            pltpu.VMEM((3, 16, 144, 256), BF16),
            pltpu.VMEM((8, TOK, D), BF16),
            pltpu.VMEM((3, SEQ, 256), BF16),
            pltpu.VMEM((SEQ, 256), BF16),
            pltpu.VMEM((8, TOK, D), BF16),
            pltpu.VMEM((2, TOK, D), BF16),
            pltpu.VMEM((4, TOK, D), BF16),
            pltpu.VMEM((TOK, D), BF16),
            pltpu.VMEM((2, FFP, D), BF16),
            dma((8,)), dma((128,)), dma((128,)), dma((8,)), dma((8,)), dma((7,)), dma((7,)),
            dma((7,)), dma((7,)), dma((8,)), dma((8,)), dma((7,)), dma((7,)), dma((2,)),
        ],
        compiler_params=pltpu.CompilerParams(collective_id=0, has_side_effects=True, vmem_limit_bytes=50 << 20),
    )(lengths, cuts, tokens, gain, freqs, tq, ow, gu)


def expert_kernel(
    len_ref, resid_ref, gain_ref, rt_ref, ids_ref, pack_ref, wt_ref, dw_ref, out_ref,
    asend, arecv, bsend, brecv, xs, ys, r1, r2, rz, hs, wo, dwo,
    asem_s, asem_r, bsem_s, bsem_r, xsem_s, xsem_r, psem_s, psem_r, csem_s, csem_r,
):
    g, i, x, zh, c, zl, y = where_am_i()
    other_core = (group_id(x, zh, 1 - c), i)
    devices = {
        "R": (group_id(lax.rem(x + 1, 4), zh, c), i),
        "L": (group_id(lax.rem(x + 3, 4), zh, c), i),
        "P": (group_id(x, 1 - zh, c), i),
    }
    barrier = pltpu.get_barrier_semaphore()
    for device in (other_core, devices["R"], devices["L"], devices["P"]):
        pl.semaphore_signal(barrier, 1, device_id=device, device_id_type=MESH)
    for k in range(1, 8):
        pl.semaphore_signal(barrier, 1, device_id=(g, lax.rem(i + k, 8)), device_id_type=MESH)

    residual = resid_ref[...]
    normed = normalize(residual, gain_ref[...]).astype(BF16)
    logits = lax.dot_general(normed, rt_ref[...], (((1,), (1,)), ((), ())), preferred_element_type=F32)
    lanes = lax.broadcasted_iota(jnp.int32, (TOK, 8), 1)
    hot = [(ids_ref[:, n:n + 1] == lanes).astype(F32) for n in range(2)]
    chosen = [jnp.sum(h * logits, axis=-1, keepdims=True) for h in hot]
    first_weight = jax.nn.sigmoid(chosen[0] - chosen[1])
    before = lax.broadcasted_iota(jnp.int32, (TOK, TOK), 1) < lax.broadcasted_iota(jnp.int32, (TOK, TOK), 0)
    ranks = jnp.dot(before.astype(BF16), (hot[0] + hot[1]).astype(BF16), preferred_element_type=F32)
    base = (lanes * SLOT).astype(F32)
    slots = lax.broadcasted_iota(jnp.int32, (TOK, 8 * SLOT), 1).astype(F32)
    pick = [(jnp.sum(h * (base + ranks), axis=-1, keepdims=True) == slots).astype(F32) for h in hot]
    rows = lax.dot_general(
        (pick[0] + pick[1]).astype(BF16), normed, (((0,), (0,)), ((), ())), preferred_element_type=F32
    )
    asend[...] = rows.astype(BF16).reshape(8, SLOT, D)
    pl.semaphore_wait(barrier, 11)

    def out_send(k):
        t = lax.rem(i + k, 8)
        return remote(asend.at[t], arecv.at[k], asem_s.at[k], asem_r.at[k], (g, t))

    for k in range(1, 8):
        out_send(k).start()
    arecv[0] = asend[i]
    core_copies = [
        remote(wt_ref, wo, csem_s.at[0], csem_r.at[0], other_core),
        remote(dw_ref, dwo, csem_s.at[1], csem_r.at[1], other_core),
    ]
    for copy in core_copies:
        copy.start()

    place = {(0, 0): (0, 0), (0, 1): (0, 1), (2, 0): (1, 0), (2, 1): (1, 1), (1, 0): (2, 0), (1, 1): (2, 1),
             (3, 0): (3, 0), (3, 1): (3, 1)}

    def make(cc):
        def block(ref):
            return lambda dx, dz: ref.at[(cc,) + place[(dx, dz)]]

        def land(k):
            return r1.at[cc, k] if k < 2 else (rz.at[cc] if k == 6 else r2.at[cc, k - 2])

        spread = Spread(block(xs), devices, (xsem_s, xsem_r), 7 * cc, True)
        gather = Gather(block(ys), land, devices, (psem_s, psem_r), 7 * cc)
        return spread, gather

    spreads, gathers = zip(*[make(cc) for cc in range(NC)])

    def pack(cc):
        rows_in = arecv[4 * cc:4 * cc + 4].reshape(4 * SLOT, D)
        packed = lax.dot_general(
            pack_ref[...], rows_in, (((1,), (0,)), ((), ())), preferred_element_type=F32
        )
        xs[cc, 0, 0] = packed.astype(BF16)

    for cc in range(NC):
        for k in range(4 * cc, 4 * cc + 4):
            if k:
                out_send(k).wait_recv()
        pack(cc)
        spreads[cc].start(0, 1, 2)

    def feed(cc, start, count):
        m = count * 2 * CH

        def up(t, carry):
            r = pl.ds(pl.multiple_of(t * 128, 128), 128)
            rows_in = xs[cc, start:start + count].reshape(m, D)
            for n, ref in enumerate((wt_ref, wo)):
                both = jnp.concatenate([ref[0, r, :], ref[1, r, :]], axis=0)
                parts = lax.dot_general(rows_in, both, (((1,), (1,)), ((), ())), preferred_element_type=F32)
                hidden = jax.nn.silu(parts[:, :128]) * parts[:, 128:]
                hs[:m, pl.ds(pl.multiple_of(n * FFP + t * 128, 128), 128)] = hidden.astype(BF16)
            return carry

        lax.fori_loop(0, 3, up, 0)

        def down(n, carry):
            cols = pl.ds(pl.multiple_of(n * 256, 256), 256)
            part = jnp.dot(hs[:m, :FFP], dw_ref[:, cols], preferred_element_type=F32)
            part = part + jnp.dot(hs[:m, FFP:], dwo[:, cols], preferred_element_type=F32)
            ys[cc, start:start + count, :, :, cols] = part.astype(BF16).reshape(count, 2, CH, 256)
            return carry

        lax.fori_loop(0, D // 256, down, 0)

    def back_send(k):
        s = lax.rem(i + 8 - k, 8)
        return remote(bsend.at[k], brecv.at[i], bsem_s.at[k], bsem_r.at[k], (g, s))

    def finish(cc):
        total = gathers[cc].total().astype(BF16)
        spaced = lax.dot_general(
            pack_ref[...], total, (((0,), (0,)), ((), ())), preferred_element_type=F32
        ).astype(BF16).reshape(4, SLOT, D)
        bsend[4 * cc:4 * cc + 4] = spaced
        for k in range(4 * cc, 4 * cc + 4):
            if k:
                back_send(k).start()
            else:
                brecv[i] = bsend[0]

    for cc in range(NC):
        spreads[cc].arrived(2)
        spreads[cc].start(3, 4)
    spreads[0].arrived(0)
    spreads[0].start(5)
    for copy in core_copies:
        copy.wait_recv()
    feed(0, 0, 1)
    spreads[0].arrived(4)
    spreads[0].start(6)
    spreads[1].arrived(0)
    spreads[1].start(5)
    spreads[0].arrived(1, 3)
    feed(0, 2, 2)
    gathers[0].start(4, 5)
    spreads[1].arrived(4)
    spreads[1].start(6)
    spreads[0].arrived(5, 6)
    feed(0, 1, 1)
    gathers[0].start(0, 1)
    feed(1, 0, 1)
    spreads[1].arrived(1, 3)
    gathers[0].middle()
    feed(1, 2, 2)
    gathers[1].start(4, 5)
    spreads[1].arrived(5, 6)
    feed(1, 1, 1)
    gathers[1].start(0, 1)
    gathers[0].cross()
    gathers[1].middle()
    finish(0)
    gathers[1].cross()
    finish(1)

    own_places = i * TOK + lax.broadcasted_iota(jnp.int32, (TOK, 1), 0)
    live = own_places < len_ref[0]
    for k in range(1, 8):
        e = lax.rem(i + k, 8)
        remote(brecv.at[e], brecv.at[e], bsem_s.at[k], bsem_r.at[k], (g, e)).wait_recv()
    flat = brecv[...].reshape(8 * SLOT, D)
    first_out = jnp.dot(pick[0].astype(BF16), flat, preferred_element_type=F32)
    second_out = jnp.dot(pick[1].astype(BF16), flat, preferred_element_type=F32)
    combined = residual + (first_weight * first_out + (1.0 - first_weight) * second_out)
    out_ref[...] = jnp.where(live, combined, 0.0).astype(BF16)

    for k in range(1, 8):
        out_send(k).wait_send()
        back_send(k).wait_send()
    for copy in core_copies:
        copy.wait_send()
    for cc in range(NC):
        spreads[cc].drain()
        gathers[cc].drain()


def experts(lengths, resid, gain, rt, ids, pack, wt, dw):
    vm = pl.BlockSpec(memory_space=pltpu.VMEM)
    sm = pl.BlockSpec(memory_space=pltpu.SMEM)
    dma = pltpu.SemaphoreType.DMA
    return pl.pallas_call(
        expert_kernel,
        name="experts",
        out_shape=jax.ShapeDtypeStruct((TOK, D), BF16),
        in_specs=[sm, vm, vm, vm, vm, vm, vm, vm],
        out_specs=vm,
        scratch_shapes=[
            pltpu.VMEM((8, SLOT, D), BF16),
            pltpu.VMEM((8, SLOT, D), BF16),
            pltpu.VMEM((8, SLOT, D), BF16),
            pltpu.VMEM((8, SLOT, D), BF16),
            pltpu.VMEM((NC, 4, 2, CH, D), BF16),
            pltpu.VMEM((NC, 4, 2, CH, D), BF16),
            pltpu.VMEM((NC, 2, CH, D), BF16),
            pltpu.VMEM((NC, 4, CH, D), BF16),
            pltpu.VMEM((NC, CH, D), BF16),
            pltpu.VMEM((4 * CH, 2 * FFP), BF16),
            pltpu.VMEM((2, FFP, D), BF16),
            pltpu.VMEM((FFP, D), BF16),
            dma((8,)), dma((8,)), dma((8,)), dma((8,)), dma((7 * NC,)), dma((7 * NC,)),
            dma((7 * NC,)), dma((7 * NC,)), dma((2,)), dma((2,)),
        ],
        compiler_params=pltpu.CompilerParams(collective_id=1, has_side_effects=True, vmem_limit_bytes=50 << 20),
    )(lengths, resid, gain, rt, ids, pack, wt, dw)


def body(
    tokens,
    lengths,
    tenant_cut,
    expert_ids,
    trainer_qkv,
    trainer_gate_up,
    out_weight,
    down_weight,
    attn_gain,
    moe_gain,
    router,
):
    half = HEAD_DIM // 2
    freqs = jnp.exp(-math.log(10000.0) * jnp.arange(half, dtype=F32) / half)
    freqs = jnp.tile(freqs, 4)[None, :]
    resid, q3, wt = front(
        tokens[0], lengths, tenant_cut, attn_gain[None, :], freqs, trainer_qkv, out_weight, trainer_gate_up
    )
    server_qkv = jnp.transpose(q3.reshape(3, D, 256), (1, 0, 2))
    server_gate_up = jnp.transpose(wt[:, :FFL, :], (2, 0, 1))[None]
    dw = jnp.pad(down_weight[0], ((0, FFP - FFL), (0, 0)))
    packed = jnp.arange(CH, dtype=jnp.int32)
    spaced = (packed // CAP) * SLOT + packed % CAP
    pack = (spaced[:, None] == jnp.arange(4 * SLOT, dtype=jnp.int32)[None, :]).astype(BF16)
    layer_out = experts(lengths, resid, moe_gain[None, :], router.T, expert_ids[0], pack, wt, dw)
    return (server_qkv, server_gate_up, layer_out[None])


def solution(mesh):
    placed = (
        P("group", "inner", None),
        P("group"),
        P("group"),
        P("group", "inner", None),
        P(("group", "inner"), None, None),
        P(None, ("group", "inner"), None, None),
        P("inner", None),
        P("inner", "group", None),
        P(),
        P(),
        P(),
    )
    return jax.shard_map(
        body,
        mesh=mesh,
        in_specs=placed,
        out_specs=(
            P(None, None, "inner"),
            P("inner", None, None, "group"),
            P("group", "inner", None),
        ),
        check_vma=False,
    )
```

```python
import math

import jax
import jax.numpy as jnp
from jax import lax
from jax.experimental import pallas as pl
from jax.experimental.pallas import tpu as pltpu
from jax.sharding import PartitionSpec as P

F32 = jnp.float32
BF16 = jnp.bfloat16
MESH = pl.DeviceIdType.MESH
D = 2304
HEAD_DIM = 64
EPS = 1e-05
MASKED = -1e30
ROWS = 18
FFL = 360
FFP = 384
CAP = 20
CH = 80
NC = 2
SEQ = 512
TOK = 64


def remote(src, dst, send_sem, recv_sem, device):
    return pltpu.make_async_remote_copy(
        src_ref=src, dst_ref=dst, send_sem=send_sem, recv_sem=recv_sem, device_id=device, device_id_type=MESH
    )


class Spread:
    SENDS = ((0, 0, "R"), (0, 0, "L"), (0, 0, "P"), (0, 1, "R"), (0, 1, "L"), (3, 0, "R"), (1, 1, "L"))
    LANDS = ((3, 0), (1, 0), (0, 1), (3, 1), (1, 1), (2, 0), (2, 1))

    def __init__(self, block, devices, sems, base, relative):
        self.block, self.devices, self.sems, self.base, self.relative = block, devices, sems, base, relative

    def send(self, k):
        dx, dz, way = self.SENDS[k]
        target = self.LANDS[k] if self.relative else (dx, dz)
        n = self.base + k
        return remote(self.block(dx, dz), self.block(*target), self.sems[0].at[n], self.sems[1].at[n], self.devices[way])

    def start(self, *ks):
        for k in ks:
            self.send(k).start()

    def arrived(self, *ks):
        for k in ks:
            n = self.base + k
            land = self.block(*self.LANDS[k])
            remote(land, land, self.sems[0].at[n], self.sems[1].at[n], self.devices[self.SENDS[k][2]]).wait_recv()

    def drain(self):
        for k in range(7):
            self.send(k).wait_send()


class Gather:
    SENDS = ((2, 0, "L"), (2, 1, "R"), (3, 0, "L"), (1, 1, "R"), (3, 1, "L"), (1, 0, "R"), (0, 1, "P"))

    def __init__(self, block, lands, devices, sems, base):
        self.block, self.lands, self.devices, self.sems, self.base = block, lands, devices, sems, base

    def send(self, k):
        dx, dz, way = self.SENDS[k]
        n = self.base + k
        return remote(self.block(dx, dz), self.lands(k), self.sems[0].at[n], self.sems[1].at[n], self.devices[way])

    def start(self, *ks):
        for k in ks:
            self.send(k).start()

    def arrived(self, *ks):
        for k in ks:
            self.send(k).wait_recv()

    def add(self, dx, dz, *ks):
        ref = self.block(dx, dz)
        total = ref[...].astype(F32)
        for k in ks:
            total = total + self.lands(k)[...].astype(F32)
        ref[...] = total.astype(BF16)

    def middle(self):
        self.arrived(0)
        self.add(3, 0, 0)
        self.start(2)
        self.arrived(1)
        self.add(1, 1, 1)
        self.start(3)

    def cross(self):
        self.arrived(3, 4)
        self.add(0, 1, 3, 4)
        self.start(6)

    def total(self):
        self.arrived(2, 5, 6)
        own = self.block(0, 0)[...].astype(F32) + self.lands(6)[...].astype(F32)
        return own + self.lands(2)[...].astype(F32) + self.lands(5)[...].astype(F32)

    def drain(self):
        for k in range(7):
            self.send(k).wait_send()


class RoutedSpread:
    ALL, TOP, LOW = (0, CH), (0, 48), (48, CH)
    STEPS = (
        ((0, 0), ALL, "R", (3, 0)),
        ((0, 0), ALL, "L", (1, 0)),
        ((0, 0), ALL, "P", (0, 1)),
        ((0, 1), ALL, "R", (3, 1)),
        ((0, 1), ALL, "L", (1, 1)),
        ((3, 0), TOP, "R", (2, 0)),
        ((1, 0), LOW, "L", (2, 0)),
        ((2, 0), TOP, "P", (2, 1)),
        ((2, 0), LOW, "P", (2, 1)),
    )

    def __init__(self, block, devices, sems, base):
        self.block, self.devices, self.sems, self.base = block, devices, sems, base

    def send(self, k):
        source, (lo, hi), way, target = self.STEPS[k]
        n = self.base + k
        return remote(
            self.block(*source).at[lo:hi], self.block(*target).at[lo:hi],
            self.sems[0].at[n], self.sems[1].at[n], self.devices[way],
        )

    def start(self, *ks):
        for k in ks:
            self.send(k).start()

    def arrived(self, *ks):
        for k in ks:
            self.send(k).wait_recv()

    def drain(self):
        for k in range(9):
            self.send(k).wait_send()


class RoutedGather:
    ALL, TOP, LOW = (0, CH), (0, 48), (48, CH)
    STEPS = (
        ((2, 1), ALL, "P", 0),
        ((2, 0), TOP, "L", 1),
        ((2, 0), LOW, "R", 1),
        ((3, 0), ALL, "L", 2),
        ((1, 0), ALL, "R", 3),
        ((3, 1), ALL, "L", 4),
        ((1, 1), ALL, "R", 5),
        ((0, 1), ALL, "P", 6),
    )

    def __init__(self, block, lands, devices, sems, base):
        self.block, self.lands, self.devices, self.sems, self.base = block, lands, devices, sems, base

    def send(self, k):
        source, (lo, hi), way, land = self.STEPS[k]
        n = self.base + k
        return remote(
            self.block(*source).at[lo:hi], self.lands(land).at[lo:hi],
            self.sems[0].at[n], self.sems[1].at[n], self.devices[way],
        )

    def start(self, *ks):
        for k in ks:
            self.send(k).start()

    def arrived(self, *ks):
        for k in ks:
            self.send(k).wait_recv()

    def add(self, place, span, *lands):
        lo, hi = span
        ref = self.block(*place).at[lo:hi]
        total = ref[...].astype(F32)
        for n in lands:
            total = total + self.lands(n).at[lo:hi][...].astype(F32)
        ref[...] = total.astype(BF16)

    def far(self):
        self.arrived(0)
        self.add((2, 0), self.TOP, 0)
        self.start(1)
        self.add((2, 0), self.LOW, 0)
        self.start(2)

    def middle(self):
        self.arrived(1)
        self.add((3, 0), self.TOP, 1)
        self.start(3)
        self.arrived(2)
        self.add((1, 0), self.LOW, 1)
        self.start(4)

    def cross(self):
        self.arrived(5, 6)
        self.add((0, 1), self.ALL, 4, 5)
        self.start(7)

    def total(self):
        self.arrived(3, 4, 7)
        total = self.block(0, 0)[...].astype(F32)
        for n in (2, 3, 6):
            total = total + self.lands(n)[...].astype(F32)
        return total

    def drain(self):
        for k in range(8):
            self.send(k).wait_send()


def where_am_i():
    g = lax.axis_index("group")
    i = lax.axis_index("inner")
    return g, i, g // 4, (g // 2) % 2, g % 2, i // 4, i % 4


def group_id(x, zh, c):
    return x * 4 + zh * 2 + c


def normalize(values, gain):
    mean_square = jnp.mean(values * values, axis=-1, keepdims=True)
    return values * lax.rsqrt(mean_square + EPS) * gain


def layer_kernel(
    len_ref, cut_ref, gain_ref, freq_ref, mgain_ref, rt_ref, ids_ref, tok_hbm, tq_hbm, ow_hbm, dw_hbm, gu_hbm,
    out_ref, q3_hbm, wt_hbm,
    tok_ref, tq_ref, ow_ref, dw_ref, resid_ref,
    gu, sbuf, rbuf, qs, qr, w, xb, qkv, att, pb, r1, r2, rz, wt,
    asend, arecv, bsend, brecv, xs, ys, lands, hs, wo, dwo,
    in_sem, load_sem, gsend, grecv, qsem_s, qsem_r, xsem_s, xsem_r, wsem_s, wsem_r, csem_s, csem_r, psem_s, psem_r,
    out_sem, asem_s, asem_r, bsem_s, bsem_r, ysem_s, ysem_r, dsem_s, dsem_r, esem_s, esem_r,
):
    g, i, x, zh, c, zl, y = where_am_i()
    me = g * 8 + i

    def load(k):
        e = lax.rem(i + k, 8)
        return pltpu.make_async_copy(gu_hbm.at[e], gu.at[k % 2], load_sem.at[k])

    parts_in = [
        pltpu.make_async_copy(tq_hbm, tq_ref, in_sem.at[0]),
        pltpu.make_async_copy(tok_hbm, tok_ref, in_sem.at[1]),
        pltpu.make_async_copy(ow_hbm, ow_ref, in_sem.at[2]),
        pltpu.make_async_copy(dw_hbm, dw_ref.at[:FFL], in_sem.at[3]),
    ]
    parts_in[1].start()
    parts_in[0].start()
    load(0).start()
    load(1).start()
    parts_in[2].start()
    parts_in[3].start()

    barrier = pltpu.get_barrier_semaphore()

    def greet(k, carry):
        t = lax.rem(me + k, 128)
        pl.semaphore_signal(barrier, 1, device_id=(t // 8, t % 8), device_id_type=MESH)
        return carry

    lax.fori_loop(1, 128, greet, 0)

    parts_in[1].wait()
    own_inputs = tok_ref[...].astype(F32)
    xb[i] = normalize(own_inputs, gain_ref[...]).astype(BF16)
    parts_in[0].wait()
    for e in range(8):
        cols = slice(e * 256, (e + 1) * 256)
        slab = jnp.concatenate([tq_ref[:, j, cols] for j in range(3)], axis=-1)
        qs[e] = slab.reshape(9, 2, 768).astype(BF16)
    pl.semaphore_wait(barrier, 127)

    inner_devices = {
        "R": (g, zl * 4 + lax.rem(y + 1, 4)),
        "L": (g, zl * 4 + lax.rem(y + 3, 4)),
        "P": (g, (1 - zl) * 4 + y),
    }
    group_devices = {
        "R": (group_id(lax.rem(x + 1, 4), zh, c), i),
        "L": (group_id(lax.rem(x + 3, 4), zh, c), i),
        "P": (group_id(x, 1 - zh, c), i),
    }

    def inner_slot(dx, dz):
        return (zl if dz == 0 else 1 - zl) * 4 + lax.rem(y + dx, 4)

    def group_slot(dx, dz):
        return group_id(lax.rem(x + dx, 4), zh if dz == 0 else 1 - zh, c)

    tokens_all = Spread(lambda dx, dz: xb.at[inner_slot(dx, dz)], inner_devices, (xsem_s, xsem_r), 0, False)
    proj_all = Spread(lambda dx, dz: w.at[:, group_slot(dx, dz)], group_devices, (wsem_s, wsem_r), 0, False)

    def slab_send(k):
        t = lax.rem(i + k, 8)
        return remote(qs.at[t], qr.at[i], qsem_s.at[k], qsem_r.at[k], (g, t))

    for k in range(1, 8):
        slab_send(k).start()
    tokens_all.start(0, 1, 2)
    qr[i] = qs[i]

    def gate_send(tg, e):
        t = tg * 8 + e
        return remote(sbuf.at[t], rbuf.at[me], gsend.at[t], grecv.at[me], (tg, e))

    def ship(k):
        e = lax.rem(i + k, 8)
        load(k).wait()
        for q in range(16):
            sbuf[q * 8 + e] = gu[k % 2, :, :, q * FFL:(q + 1) * FFL].astype(BF16)
        if k < 6:
            load(k + 2).start()

        def post(q, carry):
            tg = lax.rem(g + q, 16)
            gate_send(tg, e).start()
            return carry

        if k == 0:
            rbuf[me] = sbuf[me]
            lax.fori_loop(1, 16, post, 0)
        else:
            lax.fori_loop(0, 16, post, 0)

    ship(0)
    ship(1)
    tokens_all.arrived(2)
    tokens_all.start(3, 4)
    for k in range(1, 8):
        s = lax.rem(i + 8 - k, 8)
        remote(qr.at[s], qr.at[s], qsem_s.at[k], qsem_r.at[k], (g, s)).wait_recv()
    block = qr[...].reshape(72, 2, 768).reshape(144, 768)
    for j in range(3):
        w[j, g] = block[:, j * 256:(j + 1) * 256]
    proj_all.start(0, 1, 2)

    other_core = (group_id(x, zh, 1 - c), i)

    def core_send(k, dx, dz):
        s = group_slot(dx, dz)
        return remote(w.at[:, s], w.at[:, s], csem_s.at[k], csem_r.at[k], other_core)

    def core_land(k, dx, dz):
        s = group_id(lax.rem(x + dx, 4), zh if dz == 0 else 1 - zh, 1 - c)
        return remote(w.at[:, s], w.at[:, s], csem_s.at[k], csem_r.at[k], other_core)

    order = ((0, 0), (0, 1), (3, 0), (1, 0), (3, 1), (1, 1), (2, 0), (2, 1))
    core_send(0, 0, 0).start()
    ship(2)
    tokens_all.arrived(0)
    tokens_all.start(5)
    proj_all.arrived(2)
    proj_all.start(3, 4)
    core_send(1, 0, 1).start()
    ship(3)
    tokens_all.arrived(4)
    tokens_all.start(6)
    proj_all.arrived(0)
    proj_all.start(5)
    core_send(2, 3, 0).start()
    proj_all.arrived(1)
    core_send(3, 1, 0).start()
    ship(4)
    proj_all.arrived(4)
    proj_all.start(6)
    core_send(5, 1, 1).start()
    proj_all.arrived(3)
    core_send(4, 3, 1).start()
    ship(5)

    length = len_ref[0]
    cut = cut_ref[0]
    places = lax.broadcasted_iota(jnp.int32, (SEQ, 128), 0)
    starts = jnp.where(places >= length, length, jnp.where(places >= cut, cut, 0))
    angles = (places - starts).astype(F32) * freq_ref[...]
    cosine = jnp.cos(angles)
    lane = lax.broadcasted_iota(jnp.int32, (SEQ, 128), 1)
    early = lane % HEAD_DIM < HEAD_DIM // 2
    sine = jnp.sin(angles)
    sine = jnp.where(early, -sine, sine)

    tokens_all.arrived(1, 3, 5, 6)
    proj_all.arrived(5)
    core_send(6, 2, 0).start()
    proj_all.arrived(6)
    core_send(7, 2, 1).start()
    for k, (dx, dz) in enumerate(order):
        core_land(k, dx, dz).wait_recv()
    q3_copy = pltpu.make_async_copy(w, q3_hbm, out_sem.at[0])
    q3_copy.start()

    rows = xb[...].reshape(SEQ, D)
    for j in range(3):
        raw = jnp.dot(rows, w[j].reshape(D, 256), preferred_element_type=F32)
        if j < 2:
            halves = []
            for n in range(2):
                part = raw[:, n * 128:(n + 1) * 128]
                swapped = jnp.where(early, pltpu.roll(part, 96, 1), pltpu.roll(part, 32, 1))
                halves.append(part * cosine + swapped * sine)
            raw = jnp.concatenate(halves, axis=-1)
        qkv[j] = raw.astype(BF16)

    ship(6)
    for r in range(4):
        span = (r + 1) * 128
        t = r * 128 + lax.broadcasted_iota(jnp.int32, (128, span), 0)
        s = lax.broadcasted_iota(jnp.int32, (128, span), 1)
        seg_t = jnp.where(t >= length, 2, jnp.where(t >= cut, 1, 0))
        seg_s = jnp.where(s >= length, 2, jnp.where(s >= cut, 1, 0))
        allowed = (s <= t) & (seg_t == seg_s)
        first = lax.broadcasted_iota(jnp.int32, (128, 128), 1) < HEAD_DIM
        for n in range(2):
            cols = slice(n * 128, (n + 1) * 128)
            q = qkv[0, r * 128:(r + 1) * 128, cols]
            k = qkv[1, :span, cols]
            v = qkv[2, :span, cols]
            mixed = []
            for h in range(2):
                keep = first if h == 0 else jnp.logical_not(first)
                qh = jnp.where(keep, q.astype(F32), 0.0).astype(BF16)
                scores = lax.dot_general(qh, k, (((1,), (1,)), ((), ())), preferred_element_type=F32)
                scores = jnp.where(allowed, scores / math.sqrt(HEAD_DIM), MASKED)
                scores = jnp.exp(scores - jnp.max(scores, axis=-1, keepdims=True))
                weights = (scores / jnp.sum(scores, axis=-1, keepdims=True)).astype(BF16)
                mixed.append(jnp.dot(weights, v, preferred_element_type=F32))
            att[r * 128:(r + 1) * 128, cols] = jnp.where(first, mixed[0], mixed[1]).astype(BF16)

    parts_in[2].wait()

    def project(n, carry):
        cols = pl.ds(pl.multiple_of(n * 256, 256), 256)
        part = jnp.dot(att[...], ow_ref[:, cols], preferred_element_type=F32)
        pb[:, :, cols] = part.astype(BF16).reshape(8, TOK, 256)
        return carry

    lax.fori_loop(0, D // 256, project, 0)

    def land(k):
        return r1.at[k] if k < 2 else (rz if k == 6 else r2.at[k - 2])

    back = Gather(lambda dx, dz: pb.at[inner_slot(dx, dz)], land, inner_devices, (psem_s, psem_r), 0)
    back.start(0, 1, 4, 5)

    ship(7)
    def settle(k, carry):
        s = lax.rem(me + k, 128)
        remote(rbuf.at[s], rbuf.at[s], gsend.at[s], grecv.at[s], (s // 8, s % 8)).wait_recv()
        return carry

    wt[:, 352:384, :] = jnp.zeros((2, 32, D), BF16)
    parts_in[3].wait()
    dw_ref[FFL:] = jnp.zeros((FFP - FFL, D), BF16)


    flat = rbuf.reshape(128 * ROWS, 2, FFL)

    def turn_step(n, carry):
        cols = pl.ds(pl.multiple_of(n * 256, 256), 256)
        wt[:, :FFL, cols] = jnp.transpose(flat[cols], (1, 2, 0))
        return carry

    back.middle()
    back.cross()
    resid_ref[...] = tok_ref[...].astype(F32) + back.total()

    residual = resid_ref[...]
    normed = normalize(residual, mgain_ref[...]).astype(BF16)
    logits = lax.dot_general(normed, rt_ref[...], (((1,), (1,)), ((), ())), preferred_element_type=F32)
    lanes = lax.broadcasted_iota(jnp.int32, (TOK, 8), 1)
    hot = [(ids_ref[:, n:n + 1] == lanes).astype(F32) for n in range(2)]
    chosen = [jnp.sum(h * logits, axis=-1, keepdims=True) for h in hot]
    first_weight = jax.nn.sigmoid(chosen[0] - chosen[1])
    before = lax.broadcasted_iota(jnp.int32, (TOK, TOK), 1) < lax.broadcasted_iota(jnp.int32, (TOK, TOK), 0)
    ranks = jnp.dot(before.astype(BF16), (hot[0] + hot[1]).astype(BF16), preferred_element_type=F32)
    base = (lanes * CAP).astype(F32)
    slots = lax.broadcasted_iota(jnp.int32, (TOK, 8 * CAP), 1).astype(F32)
    pick = [(jnp.sum(h * (base + ranks), axis=-1, keepdims=True) == slots).astype(F32) for h in hot]
    rows = lax.dot_general(
        (pick[0] + pick[1]).astype(BF16), normed, (((0,), (0,)), ((), ())), preferred_element_type=F32
    )
    asend[...] = rows.reshape(8, CAP // 2, 2, D).astype(BF16)
    def out_send(k):
        t = lax.rem(i + k, 8)
        return remote(asend.at[t], arecv.at[k], asem_s.at[k], asem_r.at[k], (g, t))

    core_copies = [
        remote(wt, wo, esem_s.at[0], esem_r.at[0], other_core),
        remote(dw_ref, dwo, esem_s.at[1], esem_r.at[1], other_core),
    ]

    devices = group_devices
    place = {(0, 0): (0, 0), (0, 1): (0, 1), (2, 0): (1, 0), (2, 1): (1, 1), (1, 0): (2, 0), (1, 1): (2, 1),
             (3, 0): (3, 0), (3, 1): (3, 1)}

    def make(cc):
        def block(ref):
            return lambda dx, dz: ref.at[(cc,) + place[(dx, dz)]]

        def land(k):
            return lands.at[cc, k]

        spread = RoutedSpread(block(xs), devices, (ysem_s, ysem_r), 9 * cc)
        gather = RoutedGather(block(ys), land, devices, (dsem_s, dsem_r), 8 * cc)
        return spread, gather

    spreads, gathers = zip(*[make(cc) for cc in range(NC)])

    for k in range(1, 8):
        out_send(k).start()
    arecv[0] = asend[i]
    lax.fori_loop(1, 128, settle, 0)
    lax.fori_loop(0, 5, turn_step, 0)
    for cc in range(NC):
        for k in range(4 * cc, 4 * cc + 4):
            if k:
                out_send(k).wait_recv()
        xs[cc, 0, 0] = arecv[4 * cc:4 * cc + 4].reshape(2 * CAP, 2, D).reshape(CH, D)
        spreads[cc].start(0, 1, 2)
    lax.fori_loop(5, 9, turn_step, 0)
    for copy in core_copies:
        copy.start()
    wt_copy = pltpu.make_async_copy(wt, wt_hbm, out_sem.at[1])
    wt_copy.start()

    def feed(cc, start, count):
        m = count * 2 * CH

        def up(t, carry):
            r = pl.ds(pl.multiple_of(t * 128, 128), 128)
            rows_in = xs[cc, start:start + count].reshape(m, D)
            for n, ref in enumerate((wt, wo)):
                both = jnp.concatenate([ref[0, r, :], ref[1, r, :]], axis=0)
                parts = lax.dot_general(rows_in, both, (((1,), (1,)), ((), ())), preferred_element_type=F32)
                hidden = jax.nn.silu(parts[:, :128]) * parts[:, 128:]
                hs[:m, pl.ds(pl.multiple_of(n * FFP + t * 128, 128), 128)] = hidden.astype(BF16)
            return carry

        lax.fori_loop(0, 3, up, 0)

        def down(n, carry):
            cols = pl.ds(pl.multiple_of(n * 256, 256), 256)
            part = jnp.dot(hs[:m, :FFP], dw_ref[:, cols], preferred_element_type=F32)
            part = part + jnp.dot(hs[:m, FFP:], dwo[:, cols], preferred_element_type=F32)
            ys[cc, start:start + count, :, :, cols] = part.astype(BF16).reshape(count, 2, CH, 256)
            return carry

        lax.fori_loop(0, D // 256, down, 0)

    def back_send(k):
        s = lax.rem(i + 8 - k, 8)
        return remote(bsend.at[k], brecv.at[i], bsem_s.at[k], bsem_r.at[k], (g, s))

    def finish(cc):
        bsend[4 * cc:4 * cc + 4] = gathers[cc].total().reshape(4, CAP // 2, 2, D).astype(BF16)
        for k in range(4 * cc, 4 * cc + 4):
            if k:
                back_send(k).start()
            else:
                brecv[i] = bsend[0]

    spreads[0].arrived(2)
    spreads[0].start(3, 4)
    spreads[1].arrived(2)
    spreads[1].start(3, 4)
    spreads[0].arrived(0)
    spreads[0].start(5)
    spreads[0].arrived(1)
    spreads[0].start(6)
    spreads[1].arrived(0)
    spreads[1].start(5)
    spreads[1].arrived(1)
    spreads[1].start(6)
    spreads[0].arrived(5)
    spreads[0].start(7)
    spreads[0].arrived(6)
    spreads[0].start(8)
    for copy in core_copies:
        copy.wait_recv()
    feed(0,  0, 1)
    spreads[1].arrived(5)
    spreads[1].start(7)
    spreads[1].arrived(6)
    spreads[1].start(8)
    spreads[0].arrived(3, 4)
    feed(0,  2, 2)
    gathers[0].start(5, 6)
    spreads[0].arrived(7, 8)
    feed(0,  1, 1)
    gathers[0].start(0)
    spreads[1].arrived(7, 8)
    feed(1,  1, 1)
    gathers[1].start(0)
    gathers[0].far()
    spreads[1].arrived(3, 4)
    feed(1,  2, 2)
    gathers[1].start(5, 6)
    gathers[1].far()
    gathers[0].middle()
    feed(1,  0, 1)
    gathers[1].middle()
    gathers[0].cross()
    gathers[1].cross()
    finish(0)
    finish(1)

    own_places = i * TOK + lax.broadcasted_iota(jnp.int32, (TOK, 1), 0)
    live = own_places < len_ref[0]
    for k in range(1, 8):
        e = lax.rem(i + k, 8)
        remote(brecv.at[e], brecv.at[e], bsem_s.at[k], bsem_r.at[k], (g, e)).wait_recv()
    flat = brecv[...].reshape(4 * CAP, 2, D).reshape(8 * CAP, D)
    first_out = jnp.dot(pick[0].astype(BF16), flat, preferred_element_type=F32)
    second_out = jnp.dot(pick[1].astype(BF16), flat, preferred_element_type=F32)
    combined = resid_ref[...] + (first_weight * first_out + (1.0 - first_weight) * second_out)
    out_ref[...] = jnp.where(live, combined, 0.0).astype(BF16)

    for k in range(1, 8):
        out_send(k).wait_send()
        back_send(k).wait_send()
    for copy in core_copies:
        copy.wait_send()
    for cc in range(NC):
        spreads[cc].drain()
        gathers[cc].drain()

    def sent(k, carry):
        t = lax.rem(me + k, 128)
        gate_send(t // 8, t % 8).wait_send()
        return carry

    lax.fori_loop(1, 128, sent, 0)
    for k in range(1, 8):
        slab_send(k).wait_send()
    tokens_all.drain()
    proj_all.drain()
    back.drain()
    for k, (dx, dz) in enumerate(order):
        core_send(k, dx, dz).wait_send()
    q3_copy.wait()
    wt_copy.wait()


def layer(tokens, lengths, cuts, gain, freqs, tq, ow, gu, mgain, rt, ids, dw):
    vm = pl.BlockSpec(memory_space=pltpu.VMEM)
    sm = pl.BlockSpec(memory_space=pltpu.SMEM)
    hbm = pl.BlockSpec(memory_space=pl.ANY)
    dma = pltpu.SemaphoreType.DMA
    return pl.pallas_call(
        layer_kernel,
        name="layer",
        out_shape=(
            jax.ShapeDtypeStruct((TOK, D), BF16),
            jax.ShapeDtypeStruct((3, 16, 144, 256), BF16),
            jax.ShapeDtypeStruct((2, FFP, D), BF16),
        ),
        in_specs=[sm, sm, vm, vm, vm, vm, vm, hbm, hbm, hbm, hbm, hbm],
        out_specs=(vm, hbm, hbm),
        scratch_shapes=[
            pltpu.VMEM((TOK, D), BF16),
            pltpu.VMEM((ROWS, 3, 2048), F32),
            pltpu.VMEM((256, D), BF16),
            pltpu.VMEM((FFP, D), BF16),
            pltpu.VMEM((TOK, D), F32),
            pltpu.VMEM((2, ROWS, 2, 5760), F32),
            pltpu.VMEM((128, ROWS, 2, FFL), BF16),
            pltpu.VMEM((128, ROWS, 2, FFL), BF16),
            pltpu.VMEM((8, 9, 2, 768), BF16),
            pltpu.VMEM((8, 9, 2, 768), BF16),
            pltpu.VMEM((3, 16, 144, 256), BF16),
            pltpu.VMEM((8, TOK, D), BF16),
            pltpu.VMEM((3, SEQ, 256), BF16),
            pltpu.VMEM((SEQ, 256), BF16),
            pltpu.VMEM((8, TOK, D), BF16),
            pltpu.VMEM((2, TOK, D), BF16),
            pltpu.VMEM((4, TOK, D), BF16),
            pltpu.VMEM((TOK, D), BF16),
            pltpu.VMEM((2, FFP, D), BF16),
            pltpu.VMEM((8, CAP // 2, 2, D), BF16),
            pltpu.VMEM((8, CAP // 2, 2, D), BF16),
            pltpu.VMEM((8, CAP // 2, 2, D), BF16),
            pltpu.VMEM((8, CAP // 2, 2, D), BF16),
            pltpu.VMEM((NC, 4, 2, CH, D), BF16),
            pltpu.VMEM((NC, 4, 2, CH, D), BF16),
            pltpu.VMEM((NC, 7, CH, D), BF16),
            pltpu.VMEM((4 * CH, 2 * FFP), BF16),
            pltpu.VMEM((2, FFP, D), BF16),
            pltpu.VMEM((FFP, D), BF16),
            dma((4,)), dma((8,)), dma((128,)), dma((128,)), dma((8,)), dma((8,)), dma((7,)), dma((7,)),
            dma((7,)), dma((7,)), dma((8,)), dma((8,)), dma((7,)), dma((7,)), dma((2,)),
            dma((8,)), dma((8,)), dma((8,)), dma((8,)), dma((9 * NC,)), dma((9 * NC,)),
            dma((8 * NC,)), dma((8 * NC,)), dma((2,)), dma((2,)),
        ],
        compiler_params=pltpu.CompilerParams(collective_id=0, has_side_effects=True, vmem_limit_bytes=60 << 20),
    )(lengths, cuts, gain, freqs, mgain, rt, ids, tokens, tq, ow, dw, gu)


def body(
    tokens,
    lengths,
    tenant_cut,
    expert_ids,
    trainer_qkv,
    trainer_gate_up,
    out_weight,
    down_weight,
    attn_gain,
    moe_gain,
    router,
):
    half = HEAD_DIM // 2
    freqs = jnp.exp(-math.log(10000.0) * jnp.arange(half, dtype=F32) / half)
    freqs = jnp.tile(freqs, 4)[None, :]
    layer_out, q3, wt = layer(
        tokens[0], lengths, tenant_cut, attn_gain[None, :], freqs, trainer_qkv, out_weight, trainer_gate_up,
        moe_gain[None, :], router.T, expert_ids[0], down_weight[0],
    )
    server_qkv = jnp.transpose(q3.reshape(3, D, 256), (1, 0, 2))
    server_gate_up = jnp.transpose(wt[:, :FFL, :], (2, 0, 1))[None]
    return (server_qkv, server_gate_up, layer_out[None])


def solution(mesh):
    placed = (
        P("group", "inner", None),
        P("group"),
        P("group"),
        P("group", "inner", None),
        P(("group", "inner"), None, None),
        P(None, ("group", "inner"), None, None),
        P("inner", None),
        P("inner", "group", None),
        P(),
        P(),
        P(),
    )
    return jax.shard_map(
        body,
        mesh=mesh,
        in_specs=placed,
        out_specs=(
            P(None, None, "inner"),
            P("inner", None, None, "group"),
            P("group", "inner", None),
        ),
        check_vma=False,
    )
```

```python
import math

import jax
import jax.numpy as jnp
from jax import lax
from jax.experimental import pallas as pl
from jax.experimental.pallas import tpu as pltpu
from jax.sharding import PartitionSpec as P

F32 = jnp.float32
BF16 = jnp.bfloat16
MESH = pl.DeviceIdType.MESH
D = 2304
HEAD_DIM = 64
EPS = 1e-05
MASKED = -1e30
ROWS = 18
FFL = 360
FFP = 384
CAP = 20
CH = 80
NC = 2
SEQ = 512
TOK = 64


def remote(src, dst, send_sem, recv_sem, device):
    return pltpu.make_async_remote_copy(
        src_ref=src, dst_ref=dst, send_sem=send_sem, recv_sem=recv_sem, device_id=device, device_id_type=MESH
    )


class Spread:
    SENDS = ((0, 0, "R"), (0, 0, "L"), (0, 0, "P"), (0, 1, "R"), (0, 1, "L"), (3, 0, "R"), (1, 1, "L"))
    LANDS = ((3, 0), (1, 0), (0, 1), (3, 1), (1, 1), (2, 0), (2, 1))

    def __init__(self, block, devices, sems, base, relative):
        self.block, self.devices, self.sems, self.base, self.relative = block, devices, sems, base, relative

    def send(self, k):
        dx, dz, way = self.SENDS[k]
        target = self.LANDS[k] if self.relative else (dx, dz)
        n = self.base + k
        return remote(self.block(dx, dz), self.block(*target), self.sems[0].at[n], self.sems[1].at[n], self.devices[way])

    def start(self, *ks):
        for k in ks:
            self.send(k).start()

    def arrived(self, *ks):
        for k in ks:
            n = self.base + k
            land = self.block(*self.LANDS[k])
            remote(land, land, self.sems[0].at[n], self.sems[1].at[n], self.devices[self.SENDS[k][2]]).wait_recv()

    def drain(self):
        for k in range(7):
            self.send(k).wait_send()


class Gather:
    SENDS = ((2, 0, "L"), (2, 1, "R"), (3, 0, "L"), (1, 1, "R"), (3, 1, "L"), (1, 0, "R"), (0, 1, "P"))

    def __init__(self, block, lands, devices, sems, base):
        self.block, self.lands, self.devices, self.sems, self.base = block, lands, devices, sems, base

    def send(self, k):
        dx, dz, way = self.SENDS[k]
        n = self.base + k
        return remote(self.block(dx, dz), self.lands(k), self.sems[0].at[n], self.sems[1].at[n], self.devices[way])

    def start(self, *ks):
        for k in ks:
            self.send(k).start()

    def arrived(self, *ks):
        for k in ks:
            self.send(k).wait_recv()

    def add(self, dx, dz, *ks):
        ref = self.block(dx, dz)
        total = ref[...].astype(F32)
        for k in ks:
            total = total + self.lands(k)[...].astype(F32)
        ref[...] = total.astype(BF16)

    def middle(self):
        self.arrived(0)
        self.add(3, 0, 0)
        self.start(2)
        self.arrived(1)
        self.add(1, 1, 1)
        self.start(3)

    def cross(self):
        self.arrived(3, 4)
        self.add(0, 1, 3, 4)
        self.start(6)

    def total(self):
        self.arrived(2, 5, 6)
        own = self.block(0, 0)[...].astype(F32) + self.lands(6)[...].astype(F32)
        return own + self.lands(2)[...].astype(F32) + self.lands(5)[...].astype(F32)

    def drain(self):
        for k in range(7):
            self.send(k).wait_send()


class RoutedSpread:
    ALL, TOP, LOW = (0, CH), (0, 48), (48, CH)
    STEPS = (
        ((0, 0), ALL, "R", (3, 0)),
        ((0, 0), ALL, "L", (1, 0)),
        ((0, 0), ALL, "P", (0, 1)),
        ((0, 1), ALL, "R", (3, 1)),
        ((0, 1), ALL, "L", (1, 1)),
        ((3, 0), TOP, "R", (2, 0)),
        ((1, 0), LOW, "L", (2, 0)),
        ((2, 0), TOP, "P", (2, 1)),
        ((2, 0), LOW, "P", (2, 1)),
    )

    def __init__(self, block, devices, sems, base):
        self.block, self.devices, self.sems, self.base = block, devices, sems, base

    def send(self, k):
        source, (lo, hi), way, target = self.STEPS[k]
        n = self.base + k
        return remote(
            self.block(*source).at[lo:hi], self.block(*target).at[lo:hi],
            self.sems[0].at[n], self.sems[1].at[n], self.devices[way],
        )

    def start(self, *ks):
        for k in ks:
            self.send(k).start()

    def arrived(self, *ks):
        for k in ks:
            self.send(k).wait_recv()

    def drain(self):
        for k in range(9):
            self.send(k).wait_send()


class RoutedGather:
    ALL, TOP, LOW = (0, CH), (0, 48), (48, CH)
    STEPS = (
        ((2, 1), ALL, "P", 0),
        ((2, 0), TOP, "L", 1),
        ((2, 0), LOW, "R", 1),
        ((3, 0), ALL, "L", 2),
        ((1, 0), ALL, "R", 3),
        ((3, 1), ALL, "L", 4),
        ((1, 1), ALL, "R", 5),
        ((0, 1), ALL, "P", 6),
    )

    def __init__(self, block, lands, devices, sems, base):
        self.block, self.lands, self.devices, self.sems, self.base = block, lands, devices, sems, base

    def send(self, k):
        source, (lo, hi), way, land = self.STEPS[k]
        n = self.base + k
        return remote(
            self.block(*source).at[lo:hi], self.lands(land).at[lo:hi],
            self.sems[0].at[n], self.sems[1].at[n], self.devices[way],
        )

    def start(self, *ks):
        for k in ks:
            self.send(k).start()

    def arrived(self, *ks):
        for k in ks:
            self.send(k).wait_recv()

    def add(self, place, span, *lands):
        lo, hi = span
        ref = self.block(*place).at[lo:hi]
        total = ref[...].astype(F32)
        for n in lands:
            total = total + self.lands(n).at[lo:hi][...].astype(F32)
        ref[...] = total.astype(BF16)

    def far(self):
        self.arrived(0)
        self.add((2, 0), self.TOP, 0)
        self.start(1)
        self.add((2, 0), self.LOW, 0)
        self.start(2)

    def middle(self):
        self.arrived(1)
        self.add((3, 0), self.TOP, 1)
        self.start(3)
        self.arrived(2)
        self.add((1, 0), self.LOW, 1)
        self.start(4)

    def cross(self):
        self.arrived(5, 6)
        self.add((0, 1), self.ALL, 4, 5)
        self.start(7)

    def total(self):
        self.arrived(3, 4, 7)
        total = self.block(0, 0)[...].astype(F32)
        for n in (2, 3, 6):
            total = total + self.lands(n)[...].astype(F32)
        return total

    def drain(self):
        for k in range(8):
            self.send(k).wait_send()


def where_am_i():
    g = lax.axis_index("group")
    i = lax.axis_index("inner")
    return g, i, g // 4, (g // 2) % 2, g % 2, i // 4, i % 4


def group_id(x, zh, c):
    return x * 4 + zh * 2 + c


def normalize(values, gain):
    mean_square = jnp.mean(values * values, axis=-1, keepdims=True)
    return values * lax.rsqrt(mean_square + EPS) * gain


def layer_kernel(
    len_ref, cut_ref, gain_ref, freq_ref, mgain_ref, rt_ref, ids_ref, tok_hbm, tq_hbm, ow_hbm, dw_hbm, gu_hbm,
    out_ref, q3_hbm, wt_hbm,
    tok_ref, tq_ref, ow_ref, dw_ref, resid_ref,
    gu, sbuf, rbuf, qs, qr, w, xb, qkv, att, pb, r1, r2, rz, wt,
    asend, arecv, bsend, brecv, xs, ys, lands, hs, wo, dwo,
    in_sem, load_sem, gsend, grecv, qsem_s, qsem_r, xsem_s, xsem_r, wsem_s, wsem_r, csem_s, csem_r, psem_s, psem_r,
    out_sem, asem_s, asem_r, bsem_s, bsem_r, ysem_s, ysem_r, dsem_s, dsem_r, esem_s, esem_r,
):
    g, i, x, zh, c, zl, y = where_am_i()
    me = g * 8 + i

    def load(k):
        e = lax.rem(i + k, 8)
        return pltpu.make_async_copy(gu_hbm.at[e], gu.at[k % 2], load_sem.at[k])

    parts_in = [
        pltpu.make_async_copy(tq_hbm, tq_ref, in_sem.at[0]),
        pltpu.make_async_copy(tok_hbm, tok_ref, in_sem.at[1]),
        pltpu.make_async_copy(ow_hbm, ow_ref, in_sem.at[2]),
        pltpu.make_async_copy(dw_hbm, dw_ref.at[:FFL], in_sem.at[3]),
    ]
    parts_in[1].start()
    parts_in[0].start()
    load(0).start()
    load(1).start()
    parts_in[2].start()
    parts_in[3].start()

    barrier = pltpu.get_barrier_semaphore()

    def greet(k, carry):
        t = lax.rem(me + k, 128)
        pl.semaphore_signal(barrier, 1, device_id=(t // 8, t % 8), device_id_type=MESH)
        return carry

    lax.fori_loop(1, 128, greet, 0)

    parts_in[1].wait()
    own_inputs = tok_ref[...].astype(F32)
    xb[i] = normalize(own_inputs, gain_ref[...]).astype(BF16)
    parts_in[0].wait()
    for e in range(8):
        cols = slice(e * 256, (e + 1) * 256)
        slab = jnp.concatenate([tq_ref[:, j, cols] for j in range(3)], axis=-1)
        qs[e] = slab.reshape(9, 2, 768).astype(BF16)
    pl.semaphore_wait(barrier, 127)

    inner_devices = {
        "R": (g, zl * 4 + lax.rem(y + 1, 4)),
        "L": (g, zl * 4 + lax.rem(y + 3, 4)),
        "P": (g, (1 - zl) * 4 + y),
    }
    group_devices = {
        "R": (group_id(lax.rem(x + 1, 4), zh, c), i),
        "L": (group_id(lax.rem(x + 3, 4), zh, c), i),
        "P": (group_id(x, 1 - zh, c), i),
    }

    def inner_slot(dx, dz):
        return (zl if dz == 0 else 1 - zl) * 4 + lax.rem(y + dx, 4)

    def group_slot(dx, dz):
        return group_id(lax.rem(x + dx, 4), zh if dz == 0 else 1 - zh, c)

    tokens_all = Spread(lambda dx, dz: xb.at[inner_slot(dx, dz)], inner_devices, (xsem_s, xsem_r), 0, False)
    proj_all = Spread(lambda dx, dz: w.at[:, group_slot(dx, dz)], group_devices, (wsem_s, wsem_r), 0, False)

    def slab_send(k):
        t = lax.rem(i + k, 8)
        return remote(qs.at[t], qr.at[i], qsem_s.at[k], qsem_r.at[k], (g, t))

    for k in range(1, 8):
        slab_send(k).start()
    tokens_all.start(0, 1, 2)
    qr[i] = qs[i]

    def gate_send(tg, e):
        t = tg * 8 + e
        return remote(sbuf.at[t], rbuf.at[me], gsend.at[t], grecv.at[me], (tg, e))

    def ship(k):
        e = lax.rem(i + k, 8)
        load(k).wait()
        for q in range(16):
            sbuf[q * 8 + e] = gu[k % 2, :, :, q * FFL:(q + 1) * FFL].astype(BF16)
        if k < 6:
            load(k + 2).start()

        def post(q, carry):
            tg = lax.rem(g + 5 * q, 16)
            gate_send(tg, e).start()
            return carry

        if k == 0:
            rbuf[me] = sbuf[me]
            lax.fori_loop(1, 16, post, 0)
        else:
            lax.fori_loop(0, 16, post, 0)

    ship(0)
    ship(1)
    tokens_all.arrived(2)
    tokens_all.start(3, 4)
    for k in range(1, 8):
        s = lax.rem(i + 8 - k, 8)
        remote(qr.at[s], qr.at[s], qsem_s.at[k], qsem_r.at[k], (g, s)).wait_recv()
    block = qr[...].reshape(72, 2, 768).reshape(144, 768)
    for j in range(3):
        w[j, g] = block[:, j * 256:(j + 1) * 256]
    proj_all.start(0, 1, 2)

    other_core = (group_id(x, zh, 1 - c), i)

    def core_send(k, dx, dz):
        s = group_slot(dx, dz)
        return remote(w.at[:, s], w.at[:, s], csem_s.at[k], csem_r.at[k], other_core)

    def core_land(k, dx, dz):
        s = group_id(lax.rem(x + dx, 4), zh if dz == 0 else 1 - zh, 1 - c)
        return remote(w.at[:, s], w.at[:, s], csem_s.at[k], csem_r.at[k], other_core)

    order = ((0, 0), (0, 1), (3, 0), (1, 0), (3, 1), (1, 1), (2, 0), (2, 1))
    core_send(0, 0, 0).start()
    ship(2)
    tokens_all.arrived(0)
    tokens_all.start(5)
    proj_all.arrived(2)
    proj_all.start(3, 4)
    core_send(1, 0, 1).start()
    ship(3)
    tokens_all.arrived(4)
    tokens_all.start(6)
    proj_all.arrived(0)
    proj_all.start(5)
    core_send(2, 3, 0).start()
    proj_all.arrived(1)
    core_send(3, 1, 0).start()
    ship(4)
    proj_all.arrived(4)
    proj_all.start(6)
    core_send(5, 1, 1).start()
    proj_all.arrived(3)
    core_send(4, 3, 1).start()
    ship(5)

    length = len_ref[0]
    cut = cut_ref[0]
    places = lax.broadcasted_iota(jnp.int32, (SEQ, 128), 0)
    starts = jnp.where(places >= length, length, jnp.where(places >= cut, cut, 0))
    angles = (places - starts).astype(F32) * freq_ref[...]
    cosine = jnp.cos(angles)
    lane = lax.broadcasted_iota(jnp.int32, (SEQ, 128), 1)
    early = lane % HEAD_DIM < HEAD_DIM // 2
    sine = jnp.sin(angles)
    sine = jnp.where(early, -sine, sine)

    tokens_all.arrived(1, 3, 5, 6)
    proj_all.arrived(5)
    core_send(6, 2, 0).start()
    proj_all.arrived(6)
    core_send(7, 2, 1).start()
    for k, (dx, dz) in enumerate(order):
        core_land(k, dx, dz).wait_recv()
    q3_copy = pltpu.make_async_copy(w, q3_hbm, out_sem.at[0])
    q3_copy.start()

    rows = xb[...].reshape(SEQ, D)
    for j in range(3):
        raw = jnp.dot(rows, w[j].reshape(D, 256), preferred_element_type=F32)
        if j < 2:
            halves = []
            for n in range(2):
                part = raw[:, n * 128:(n + 1) * 128]
                swapped = jnp.where(early, pltpu.roll(part, 96, 1), pltpu.roll(part, 32, 1))
                halves.append(part * cosine + swapped * sine)
            raw = jnp.concatenate(halves, axis=-1)
        qkv[j] = raw.astype(BF16)

    ship(6)
    for r in range(4):
        span = (r + 1) * 128
        t = r * 128 + lax.broadcasted_iota(jnp.int32, (128, span), 0)
        s = lax.broadcasted_iota(jnp.int32, (128, span), 1)
        seg_t = jnp.where(t >= length, 2, jnp.where(t >= cut, 1, 0))
        seg_s = jnp.where(s >= length, 2, jnp.where(s >= cut, 1, 0))
        allowed = (s <= t) & (seg_t == seg_s)
        first = lax.broadcasted_iota(jnp.int32, (128, 128), 1) < HEAD_DIM
        for n in range(2):
            cols = slice(n * 128, (n + 1) * 128)
            q = qkv[0, r * 128:(r + 1) * 128, cols]
            k = qkv[1, :span, cols]
            v = qkv[2, :span, cols]
            mixed = []
            for h in range(2):
                keep = first if h == 0 else jnp.logical_not(first)
                qh = jnp.where(keep, q.astype(F32), 0.0).astype(BF16)
                scores = lax.dot_general(qh, k, (((1,), (1,)), ((), ())), preferred_element_type=F32)
                scores = jnp.where(allowed, scores / math.sqrt(HEAD_DIM), MASKED)
                scores = jnp.exp(scores - jnp.max(scores, axis=-1, keepdims=True))
                weights = (scores / jnp.sum(scores, axis=-1, keepdims=True)).astype(BF16)
                mixed.append(jnp.dot(weights, v, preferred_element_type=F32))
            att[r * 128:(r + 1) * 128, cols] = jnp.where(first, mixed[0], mixed[1]).astype(BF16)

    parts_in[2].wait()

    def project(n, carry):
        cols = pl.ds(pl.multiple_of(n * 256, 256), 256)
        part = jnp.dot(att[...], ow_ref[:, cols], preferred_element_type=F32)
        pb[:, :, cols] = part.astype(BF16).reshape(8, TOK, 256)
        return carry

    lax.fori_loop(0, D // 256, project, 0)

    def land(k):
        return r1.at[k] if k < 2 else (rz if k == 6 else r2.at[k - 2])

    back = Gather(lambda dx, dz: pb.at[inner_slot(dx, dz)], land, inner_devices, (psem_s, psem_r), 0)
    back.start(0, 1, 4, 5)

    ship(7)
    def settle(k, carry):
        s = lax.rem(me + k, 128)
        remote(rbuf.at[s], rbuf.at[s], gsend.at[s], grecv.at[s], (s // 8, s % 8)).wait_recv()
        return carry

    wt[:, 352:384, :] = jnp.zeros((2, 32, D), BF16)
    parts_in[3].wait()
    dw_ref[FFL:] = jnp.zeros((FFP - FFL, D), BF16)


    flat = rbuf.reshape(128 * ROWS, 2, FFL)

    def turn_step(n, carry):
        cols = pl.ds(pl.multiple_of(n * 256, 256), 256)
        wt[:, :FFL, cols] = jnp.transpose(flat[cols], (1, 2, 0))
        return carry

    back.middle()
    back.cross()
    resid_ref[...] = tok_ref[...].astype(F32) + back.total()

    residual = resid_ref[...]
    normed = normalize(residual, mgain_ref[...]).astype(BF16)
    logits = lax.dot_general(normed, rt_ref[...], (((1,), (1,)), ((), ())), preferred_element_type=F32)
    lanes = lax.broadcasted_iota(jnp.int32, (TOK, 8), 1)
    hot = [(ids_ref[:, n:n + 1] == lanes).astype(F32) for n in range(2)]
    chosen = [jnp.sum(h * logits, axis=-1, keepdims=True) for h in hot]
    first_weight = jax.nn.sigmoid(chosen[0] - chosen[1])
    before = lax.broadcasted_iota(jnp.int32, (TOK, TOK), 1) < lax.broadcasted_iota(jnp.int32, (TOK, TOK), 0)
    ranks = jnp.dot(before.astype(BF16), (hot[0] + hot[1]).astype(BF16), preferred_element_type=F32)
    base = (lanes * CAP).astype(F32)
    slots = lax.broadcasted_iota(jnp.int32, (TOK, 8 * CAP), 1).astype(F32)
    pick = [(jnp.sum(h * (base + ranks), axis=-1, keepdims=True) == slots).astype(F32) for h in hot]
    rows = lax.dot_general(
        (pick[0] + pick[1]).astype(BF16), normed, (((0,), (0,)), ((), ())), preferred_element_type=F32
    )
    asend[...] = rows.reshape(8, CAP // 2, 2, D).astype(BF16)
    def out_send(k):
        t = lax.rem(i + k, 8)
        return remote(asend.at[t], arecv.at[k], asem_s.at[k], asem_r.at[k], (g, t))

    core_copies = [
        remote(wt, wo, esem_s.at[0], esem_r.at[0], other_core),
        remote(dw_ref, dwo, esem_s.at[1], esem_r.at[1], other_core),
    ]

    devices = group_devices
    place = {(0, 0): (0, 0), (0, 1): (0, 1), (2, 0): (1, 0), (2, 1): (1, 1), (1, 0): (2, 0), (1, 1): (2, 1),
             (3, 0): (3, 0), (3, 1): (3, 1)}

    def make(cc):
        def block(ref):
            return lambda dx, dz: ref.at[(cc,) + place[(dx, dz)]]

        def land(k):
            return lands.at[cc, k]

        spread = RoutedSpread(block(xs), devices, (ysem_s, ysem_r), 9 * cc)
        gather = RoutedGather(block(ys), land, devices, (dsem_s, dsem_r), 8 * cc)
        return spread, gather

    spreads, gathers = zip(*[make(cc) for cc in range(NC)])

    for k in range(1, 8):
        out_send(k).start()
    arecv[0] = asend[i]
    for cc in range(NC):
        for k in range(4 * cc, 4 * cc + 4):
            if k:
                out_send(k).wait_recv()
        xs[cc, 0, 0] = arecv[4 * cc:4 * cc + 4].reshape(2 * CAP, 2, D).reshape(CH, D)
        spreads[cc].start(0, 1, 2)
    lax.fori_loop(1, 128, settle, 0)
    lax.fori_loop(0, 5, turn_step, 0)

    def feed(cc, start, count):
        m = count * 2 * CH

        def up(t, carry):
            r = pl.ds(pl.multiple_of(t * 128, 128), 128)
            rows_in = xs[cc, start:start + count].reshape(m, D)
            for n, ref in enumerate((wt, wo)):
                both = jnp.concatenate([ref[0, r, :], ref[1, r, :]], axis=0)
                parts = lax.dot_general(rows_in, both, (((1,), (1,)), ((), ())), preferred_element_type=F32)
                hidden = jax.nn.silu(parts[:, :128]) * parts[:, 128:]
                hs[:m, pl.ds(pl.multiple_of(n * FFP + t * 128, 128), 128)] = hidden.astype(BF16)
            return carry

        lax.fori_loop(0, 3, up, 0)

        def down(n, carry):
            cols = pl.ds(pl.multiple_of(n * 256, 256), 256)
            part = jnp.dot(hs[:m, :FFP], dw_ref[:, cols], preferred_element_type=F32)
            part = part + jnp.dot(hs[:m, FFP:], dwo[:, cols], preferred_element_type=F32)
            ys[cc, start:start + count, :, :, cols] = part.astype(BF16).reshape(count, 2, CH, 256)
            return carry

        lax.fori_loop(0, D // 256, down, 0)

    def back_send(k):
        s = lax.rem(i + 8 - k, 8)
        return remote(bsend.at[k], brecv.at[i], bsem_s.at[k], bsem_r.at[k], (g, s))

    def finish(cc):
        bsend[4 * cc:4 * cc + 4] = gathers[cc].total().reshape(4, CAP // 2, 2, D).astype(BF16)
        for k in range(4 * cc, 4 * cc + 4):
            if k:
                back_send(k).start()
            else:
                brecv[i] = bsend[0]

    spreads[0].arrived(2)
    spreads[0].start(3, 4)
    lax.fori_loop(5, 9, turn_step, 0)
    for copy in core_copies:
        copy.start()
    wt_copy = pltpu.make_async_copy(wt, wt_hbm, out_sem.at[1])
    wt_copy.start()
    spreads[0].arrived(0)
    spreads[0].start(5)
    spreads[0].arrived(1)
    spreads[0].start(6)
    spreads[1].arrived(2)
    spreads[1].start(3, 4)
    spreads[1].arrived(0)
    spreads[1].start(5)
    spreads[1].arrived(1)
    spreads[1].start(6)
    spreads[0].arrived(5)
    spreads[0].start(7)
    spreads[0].arrived(6)
    spreads[0].start(8)
    for copy in core_copies:
        copy.wait_recv()
    feed(0,  0, 1)
    spreads[1].arrived(5)
    spreads[1].start(7)
    spreads[1].arrived(6)
    spreads[1].start(8)
    spreads[0].arrived(3, 4)
    feed(0,  2, 2)
    gathers[0].start(5, 6)
    spreads[0].arrived(7, 8)
    feed(0,  1, 1)
    gathers[0].start(0)
    spreads[1].arrived(7, 8)
    feed(1,  1, 1)
    gathers[1].start(0)
    gathers[0].far()
    spreads[1].arrived(3, 4)
    feed(1,  2, 2)
    gathers[1].start(5, 6)
    gathers[1].far()
    gathers[0].middle()
    feed(1,  0, 1)
    gathers[1].middle()
    gathers[0].cross()
    gathers[1].cross()
    finish(0)
    finish(1)

    own_places = i * TOK + lax.broadcasted_iota(jnp.int32, (TOK, 1), 0)
    live = own_places < len_ref[0]
    for k in range(1, 8):
        e = lax.rem(i + k, 8)
        remote(brecv.at[e], brecv.at[e], bsem_s.at[k], bsem_r.at[k], (g, e)).wait_recv()
    flat = brecv[...].reshape(4 * CAP, 2, D).reshape(8 * CAP, D)
    first_out = jnp.dot(pick[0].astype(BF16), flat, preferred_element_type=F32)
    second_out = jnp.dot(pick[1].astype(BF16), flat, preferred_element_type=F32)
    combined = resid_ref[...] + (first_weight * first_out + (1.0 - first_weight) * second_out)
    out_ref[...] = jnp.where(live, combined, 0.0).astype(BF16)

    for k in range(1, 8):
        out_send(k).wait_send()
        back_send(k).wait_send()
    for copy in core_copies:
        copy.wait_send()
    for cc in range(NC):
        spreads[cc].drain()
        gathers[cc].drain()

    def sent(k, carry):
        t = lax.rem(me + k, 128)
        gate_send(t // 8, t % 8).wait_send()
        return carry

    lax.fori_loop(1, 128, sent, 0)
    for k in range(1, 8):
        slab_send(k).wait_send()
    tokens_all.drain()
    proj_all.drain()
    back.drain()
    for k, (dx, dz) in enumerate(order):
        core_send(k, dx, dz).wait_send()
    q3_copy.wait()
    wt_copy.wait()


def layer(tokens, lengths, cuts, gain, freqs, tq, ow, gu, mgain, rt, ids, dw):
    vm = pl.BlockSpec(memory_space=pltpu.VMEM)
    sm = pl.BlockSpec(memory_space=pltpu.SMEM)
    hbm = pl.BlockSpec(memory_space=pl.ANY)
    dma = pltpu.SemaphoreType.DMA
    return pl.pallas_call(
        layer_kernel,
        name="layer",
        out_shape=(
            jax.ShapeDtypeStruct((TOK, D), BF16),
            jax.ShapeDtypeStruct((3, 16, 144, 256), BF16),
            jax.ShapeDtypeStruct((2, FFP, D), BF16),
        ),
        in_specs=[sm, sm, vm, vm, vm, vm, vm, hbm, hbm, hbm, hbm, hbm],
        out_specs=(vm, hbm, hbm),
        scratch_shapes=[
            pltpu.VMEM((TOK, D), BF16),
            pltpu.VMEM((ROWS, 3, 2048), F32),
            pltpu.VMEM((256, D), BF16),
            pltpu.VMEM((FFP, D), BF16),
            pltpu.VMEM((TOK, D), F32),
            pltpu.VMEM((2, ROWS, 2, 5760), F32),
            pltpu.VMEM((128, ROWS, 2, FFL), BF16),
            pltpu.VMEM((128, ROWS, 2, FFL), BF16),
            pltpu.VMEM((8, 9, 2, 768), BF16),
            pltpu.VMEM((8, 9, 2, 768), BF16),
            pltpu.VMEM((3, 16, 144, 256), BF16),
            pltpu.VMEM((8, TOK, D), BF16),
            pltpu.VMEM((3, SEQ, 256), BF16),
            pltpu.VMEM((SEQ, 256), BF16),
            pltpu.VMEM((8, TOK, D), BF16),
            pltpu.VMEM((2, TOK, D), BF16),
            pltpu.VMEM((4, TOK, D), BF16),
            pltpu.VMEM((TOK, D), BF16),
            pltpu.VMEM((2, FFP, D), BF16),
            pltpu.VMEM((8, CAP // 2, 2, D), BF16),
            pltpu.VMEM((8, CAP // 2, 2, D), BF16),
            pltpu.VMEM((8, CAP // 2, 2, D), BF16),
            pltpu.VMEM((8, CAP // 2, 2, D), BF16),
            pltpu.VMEM((NC, 4, 2, CH, D), BF16),
            pltpu.VMEM((NC, 4, 2, CH, D), BF16),
            pltpu.VMEM((NC, 7, CH, D), BF16),
            pltpu.VMEM((4 * CH, 2 * FFP), BF16),
            pltpu.VMEM((2, FFP, D), BF16),
            pltpu.VMEM((FFP, D), BF16),
            dma((4,)), dma((8,)), dma((128,)), dma((128,)), dma((8,)), dma((8,)), dma((7,)), dma((7,)),
            dma((7,)), dma((7,)), dma((8,)), dma((8,)), dma((7,)), dma((7,)), dma((2,)),
            dma((8,)), dma((8,)), dma((8,)), dma((8,)), dma((9 * NC,)), dma((9 * NC,)),
            dma((8 * NC,)), dma((8 * NC,)), dma((2,)), dma((2,)),
        ],
        compiler_params=pltpu.CompilerParams(collective_id=0, has_side_effects=True, vmem_limit_bytes=60 << 20),
    )(lengths, cuts, gain, freqs, mgain, rt, ids, tokens, tq, ow, dw, gu)


def body(
    tokens,
    lengths,
    tenant_cut,
    expert_ids,
    trainer_qkv,
    trainer_gate_up,
    out_weight,
    down_weight,
    attn_gain,
    moe_gain,
    router,
):
    half = HEAD_DIM // 2
    freqs = jnp.exp(-math.log(10000.0) * jnp.arange(half, dtype=F32) / half)
    freqs = jnp.tile(freqs, 4)[None, :]
    layer_out, q3, wt = layer(
        tokens[0], lengths, tenant_cut, attn_gain[None, :], freqs, trainer_qkv, out_weight, trainer_gate_up,
        moe_gain[None, :], router.T, expert_ids[0], down_weight[0],
    )
    server_qkv = jnp.transpose(q3.reshape(3, D, 256), (1, 0, 2))
    server_gate_up = jnp.transpose(wt[:, :FFL, :], (2, 0, 1))[None]
    return (server_qkv, server_gate_up, layer_out[None])


def solution(mesh):
    placed = (
        P("group", "inner", None),
        P("group"),
        P("group"),
        P("group", "inner", None),
        P(("group", "inner"), None, None),
        P(None, ("group", "inner"), None, None),
        P("inner", None),
        P("inner", "group", None),
        P(),
        P(),
        P(),
    )
    return jax.shard_map(
        body,
        mesh=mesh,
        in_specs=placed,
        out_specs=(
            P(None, None, "inner"),
            P("inner", None, None, "group"),
            P("group", "inner", None),
        ),
        check_vma=False,
    )
```
